128 devices in a mesh: gx: 8 (over y, core), gy: 16 (over z, x).
Axes of the slice: x: 4, y: 4, z: 4, core: 2. Of those that a mesh axis runs over, the one named last changes fastest.
Arguments:
- interface_conditions: float32 [8, 1024, 2048], P(None, 'gx', 'gy'), may hold values from -3 to 1.5, as said below
- level_warmth_profile: float32 [4096, 5, 10, 1024], P(('gx', 'gy')), may hold values from -2 to -0.1
- class_coverage_share: float32 [4096, 5, 1024], P(('gx', 'gy')), may hold values from 0.02 to 0.4
- class_floe_depth: float32 [4096, 5, 1024], P(('gx', 'gy')), may hold values from 0.5 to 4
- class_drift_depth: float32 [4096, 5, 1024], P(('gx', 'gy')), may hold values from 0.05 to 0.5
- floe_drift_speed: float32 [2, 1024, 2048], P(None, 'gx', 'gy'), may hold values from -3 to 3
- internal_tension_tensor: float32 [3, 1024, 2048], P(None, 'gx', 'gy'), may hold values from -3 to 3
- external_drive: float32 [4, 1024, 2048], P(None, 'gx', 'gy'), may hold values from -2 to 2
- floe_weight: float32 [1024, 2048], P('gx', 'gy'), may hold values from 0.3 to 3
- floe_pressure: float32 [1024, 2048], P('gx', 'gy'), may hold values from 0.2 to 2
- holder_lookup: int32 [2048, 1], P(('gx', 'gy')), may hold values from 0 to 15, as said below
- ground_tile_marker: int32 [2048], P(('gx', 'gy')), may hold values from 0 to 1, as said below
Outputs:
- revised_level_warmth: float32 [4096, 5, 10, 1024], P(('gx', 'gy'))
- interface_exchanges: float32 [8, 1024, 2048], P(None, 'gx', 'gy')
- velocity_new: float32 [2, 1024, 2048], P(None, 'gx', 'gy')
- stress_new: float32 [3, 1024, 2048], P(None, 'gx', 'gy')
The draws below stay inside these ranges and needn't reach their ends.
Inputs may be any that keep to these rules, and one draw needn't show every extreme that they name: `interface_conditions`: fields in order: ocean temperature in -0.2 to 0.1, salinity in 0.5 to 1, air temperature in -3 to -0.2, visible and near-infrared shortwave in 0 to 1, longwave in 0.5 to 1.5, snowfall and wind speed in 0 to 1. `holder_lookup`: each tile names one owner for at most 2 of its blocks. In every row of tiles there is one owner that every tile of the row names for exactly 2 blocks, none of them land. `ground_tile_marker`: 1 marks a land block.
All inputs are finite; a program needn't handle non-finite values.
Results may differ from the reference program's by a relative error of at most 0.0003.
Values sent between devices are 32-bit elements; how exact they have to be, the bound alone decides.
No kernel may reach another device: no remote copies, remote signals or barrier semaphores. Data moves between devices by JAX's collectives and lax.ppermute only.
A program may use at most 128 MiB of HBM per device.

```python
import math
import jax
import jax.numpy as jnp
from jax import lax

BS = 32
BPX = 4
BPY = 4
CAP = 2
DEPTH_CLASSES = 5
FROZEN_LEVELS = 7
DRIFT_LEVELS = 3
POINT_QUANTITIES = 8
SUB = 4
TILE_POINTS = 1024
B = 16
HOLDER_PLACES = 32
NX = 1024
NY = 2048
GRID_BLOCK_COUNT = 2048
HOLDER_POSITIONS = 4096
N_GX = 8
N_GY = 16


def draw_interface_conditions(key, part):
    lower_ends = jnp.array([-0.2, 0.5, -3.0, 0.0, 0.0, 0.5, 0.0, 0.0], jnp.float32)
    upper_ends = jnp.array([0.1, 1.0, -0.2, 1.0, 1.0, 1.5, 1.0, 1.0], jnp.float32)
    unit_draw = jax.random.uniform(key, (POINT_QUANTITIES, NX, NY), jnp.float32)
    return lower_ends[:, None, None] + (upper_ends - lower_ends)[:, None, None] * unit_draw


def route_plan(key):
    base_key = jax.random.fold_in(key, 11)
    pick_key, place_key, land_key = jax.random.split(base_key, 3)
    device_count = N_GX * N_GY
    favoured = jax.random.randint(pick_key, (N_GX,), 0, N_GY)
    favoured_dev = jnp.repeat(favoured, N_GY)
    entry_owner = jnp.arange(N_GY * CAP, dtype=jnp.int32) // CAP

    def one_device(device_key, chosen):
        first_key, second_key = jax.random.split(device_key)
        shuffled = jax.random.permutation(first_key, entry_owner)
        pushed = (shuffled == chosen).astype(jnp.int32)
        arranged = shuffled[jnp.argsort(pushed, stable=True)]
        listed = jnp.concatenate([jnp.full((CAP,), chosen, jnp.int32), arranged[:B - CAP]])
        return jax.random.permutation(second_key, listed)
    owners = jax.vmap(one_device)(jax.random.split(place_key, device_count), favoured_dev)
    land_flag = (jax.random.randint(land_key, (device_count, B), 0, 4) == 0) & (owners != favoured_dev[:, None])
    return (owners.reshape(GRID_BLOCK_COUNT, 1).astype(jnp.int32), land_flag.astype(jnp.int32).reshape(GRID_BLOCK_COUNT))


def draw_holder_lookup(key, part):
    return route_plan(key)[0]


def draw_ground_tile_marker(key, part):
    return route_plan(key)[1]


def steps_of(stream_key, extent, cuts, low, top_value):
    loudness = 1.0
    for axis_at, parts in cuts:
        steps = jax.random.uniform(jax.random.fold_in(jax.random.fold_in(stream_key, 6), axis_at), (parts,), jnp.float32, low / len(cuts), top_value / len(cuts))
        loudness = loudness * jnp.repeat(jnp.exp(steps), extent[axis_at] // parts).reshape((-1,) + (1,) * (len(extent) - 1 - axis_at))
    return loudness


def centred(key, shape, scale, limit, pieces=(), kind=jnp.bfloat16):
    result = scale * jax.random.normal(key, shape, jnp.float32)
    if pieces:
        result = result * steps_of(key, shape, pieces, -0.22, 0.18)
    return jnp.clip(result, -limit, limit).astype(kind)


def setup_inputs(seed: int = 0) -> dict:
    seeds = jax.random.split(jax.random.key(seed), 13)
    return {
        "interface_conditions": draw_interface_conditions(jax.random.fold_in(seeds[12], 71), 0),
        "level_warmth_profile": jnp.clip(-2.0 + 1.9 * jax.random.uniform(seeds[1], (HOLDER_POSITIONS, DEPTH_CLASSES, DRIFT_LEVELS + FROZEN_LEVELS, TILE_POINTS), jnp.float32) ** steps_of(seeds[1], (HOLDER_POSITIONS, DEPTH_CLASSES, DRIFT_LEVELS + FROZEN_LEVELS, TILE_POINTS), ((0, 128),), -0.2, 0.2), -2.0, -0.1),
        "class_coverage_share": jnp.clip(0.02 + 0.38 * jax.random.uniform(seeds[2], (HOLDER_POSITIONS, DEPTH_CLASSES, TILE_POINTS), jnp.float32) ** steps_of(seeds[2], (HOLDER_POSITIONS, DEPTH_CLASSES, TILE_POINTS), ((0, 128),), -0.2, 0.2), 0.02, 0.4),
        "class_floe_depth": jnp.clip(jnp.exp(math.log(4.0) - 2.0794415 * jax.random.uniform(seeds[3], (HOLDER_POSITIONS, DEPTH_CLASSES, TILE_POINTS), jnp.float32) ** steps_of(seeds[3], (HOLDER_POSITIONS, DEPTH_CLASSES, TILE_POINTS), ((0, 128),), -0.2, 0.2)), 0.5, 4.0),
        "class_drift_depth": jnp.clip(jnp.exp(math.log(0.5) - 2.3025851 * jax.random.uniform(seeds[4], (HOLDER_POSITIONS, DEPTH_CLASSES, TILE_POINTS), jnp.float32) ** steps_of(seeds[4], (HOLDER_POSITIONS, DEPTH_CLASSES, TILE_POINTS), ((0, 128),), -0.2, 0.2)), 0.05, 0.5),
        "floe_drift_speed": centred(seeds[5], (2, NX, NY), 0.5, 3.0, ((1, 8), (2, 16)), jnp.float32),
        "internal_tension_tensor": centred(seeds[6], (3, NX, NY), 0.5, 3.0, ((1, 8), (2, 16)), jnp.float32),
        "external_drive": centred(seeds[7], (4, NX, NY), 0.3, 2.0, ((1, 8), (2, 16)), jnp.float32),
        "floe_weight": jnp.clip(jnp.exp(math.log(3.0) - 2.3025851 * jax.random.uniform(seeds[8], (NX, NY), jnp.float32) ** steps_of(seeds[8], (NX, NY), ((0, 8), (1, 16)), -0.2, 0.2)), 0.3, 3.0),
        "floe_pressure": jnp.clip(jnp.exp(math.log(2.0) - 2.3025851 * jax.random.uniform(seeds[9], (NX, NY), jnp.float32) ** steps_of(seeds[9], (NX, NY), ((0, 8), (1, 16)), -0.2, 0.2)), 0.2, 2.0),
        "holder_lookup": draw_holder_lookup(jax.random.fold_in(seeds[12], 71), 0),
        "ground_tile_marker": draw_ground_tile_marker(jax.random.fold_in(seeds[12], 71), 0),
    }


RELAX_RATE = 0.5
ECC_SQUARED = 4.0
DELTA_FLOOR = 0.04
MOTION_STEP = 0.5
WATER_DRAG = 1.0
CORIOLIS = 0.3
HEAT_STEP = 0.5
SNOW_COND = 0.3
SNOW_GAIN = 0.3
GROWTH_RATE = 0.05

def column_step(layer_temp, cat_area, cat_thick, cat_snow, forcing_fields):
    ocean_temp = forcing_fields[:, 0:1]
    salinity = forcing_fields[:, 1:2]
    air_temp = forcing_fields[:, 2:3]
    visible = forcing_fields[:, 3:4]
    near_red = forcing_fields[:, 4:5]
    longwave = forcing_fields[:, 5:6]
    snowfall = forcing_fields[:, 6:7]
    wind_speed = forcing_fields[:, 7:8]
    snow_depth = cat_snow + SNOW_GAIN * snowfall
    layer_total = DRIFT_LEVELS + FROZEN_LEVELS
    depths = []
    heat_caps = []
    resist = []
    for layer_num in range(layer_total):
        old_temp = layer_temp[:, :, layer_num]
        if layer_num < DRIFT_LEVELS:
            layer_depth = snow_depth / DRIFT_LEVELS
            heat_cap = jnp.ones_like(layer_depth)
            conduct = SNOW_COND
        else:
            brine_term = salinity * (0.2 + 0.1 * (layer_num - DRIFT_LEVELS))
            layer_depth = cat_thick / FROZEN_LEVELS
            heat_cap = 1.0 + 0.2 * brine_term / (old_temp * old_temp + 0.1)
            conduct = 2.0 + 0.1 * brine_term / (old_temp - 0.5)
        depths.append(layer_depth)
        heat_caps.append(heat_cap)
        resist.append(layer_depth / conduct)
    top_cond = 1.0 / (0.5 * resist[0] + 1.0 / (1.0 + 2.0 * wind_speed))
    bottom_cond = 2.0 / resist[-1]
    inner_cond = [1.0 / (0.5 * (resist[layer_num] + resist[layer_num + 1])) for layer_num in range(layer_total - 1)]
    cond_above = [top_cond] + inner_cond
    cond_below = inner_cond + [bottom_cond]
    sweep_ratio = []
    sweep_value = []
    for layer_num in range(layer_total):
        mass_term = heat_caps[layer_num] * depths[layer_num] / HEAT_STEP
        diagonal = mass_term + cond_above[layer_num] + cond_below[layer_num]
        source = mass_term * layer_temp[:, :, layer_num]
        if layer_num == 0:
            source = source + top_cond * air_temp + 0.25 * visible + 0.45 * near_red + 0.3 * longwave
        if layer_num == layer_total - 1:
            source = source + bottom_cond * ocean_temp
        if layer_num > 0:
            pivot_term = diagonal - cond_above[layer_num] * sweep_ratio[-1]
            carried = source + cond_above[layer_num] * sweep_value[-1]
        else:
            pivot_term = diagonal
            carried = source
        sweep_ratio.append(cond_below[layer_num] / pivot_term)
        sweep_value.append(carried / pivot_term)
    solved = [sweep_value[-1]]
    for layer_num in range(layer_total - 2, -1, -1):
        solved.insert(0, sweep_value[layer_num] + sweep_ratio[layer_num] * solved[0])
    advanced_warmth = jnp.stack(solved, axis=2)
    bottom_flux = bottom_cond * (solved[-1] - ocean_temp)
    growth = -GROWTH_RATE * bottom_flux
    energy = heat_caps[0] * depths[0] * solved[0]
    for layer_num in range(1, layer_total):
        energy = energy + heat_caps[layer_num] * depths[layer_num] * solved[layer_num]
    light_through = 0.7 * visible * jnp.exp(-5.0 * snow_depth - 1.5 * cat_thick)
    flux_terms = [bottom_flux, top_cond * (air_temp - solved[0]), light_through, solved[0], snow_depth, cat_thick + growth, 0.1 * energy, growth * salinity]
    slot_fluxes = jnp.stack([lax.optimization_barrier(jnp.sum(cat_area * term_value, axis=1)) for term_value in flux_terms], axis=1)
    return (advanced_warmth, slot_fluxes)

def strain_rates(drift_kinematics):
    east_vel = drift_kinematics[0]
    north_vel = drift_kinematics[1]
    du_x = 0.5 * (east_vel[2:, 1:-1] - east_vel[:-2, 1:-1])
    du_y = 0.5 * (east_vel[1:-1, 2:] - east_vel[1:-1, :-2])
    dv_x = 0.5 * (north_vel[2:, 1:-1] - north_vel[:-2, 1:-1])
    dv_y = 0.5 * (north_vel[1:-1, 2:] - north_vel[1:-1, :-2])
    return (du_x + dv_y, du_x - dv_y, du_y + dv_x)

def update_stress(stress_old, strength, drift_kinematics):
    diverge, tension, shearing = strain_rates(drift_kinematics)
    spread = jnp.sqrt(diverge * diverge + (tension * tension + shearing * shearing) / ECC_SQUARED + DELTA_FLOOR)
    ratio = strength / spread
    first = (stress_old[0] + RELAX_RATE * ratio * (diverge - spread)) / (1.0 + RELAX_RATE)
    second = (stress_old[1] + RELAX_RATE * ratio * tension / ECC_SQUARED) / (1.0 + RELAX_RATE)
    third = (stress_old[2] + RELAX_RATE * ratio * shearing / (2.0 * ECC_SQUARED)) / (1.0 + RELAX_RATE)
    return jnp.stack([first, second, third])

def stress_force(stress_pad):
    stress_sum = stress_pad[0] + stress_pad[1]
    differ = stress_pad[0] - stress_pad[1]
    shear_part = stress_pad[2]
    force_x = 0.25 * (stress_sum[2:, 1:-1] - stress_sum[:-2, 1:-1]) + 0.5 * (shear_part[1:-1, 2:] - shear_part[1:-1, :-2])
    force_y = 0.25 * (differ[1:-1, 2:] - differ[1:-1, :-2]) + 0.5 * (shear_part[2:, 1:-1] - shear_part[:-2, 1:-1])
    return (force_x, force_y)

def update_motion(drift_kinematics, force_x, force_y, floe_weight, external_drive, water_mask):
    east_vel = drift_kinematics[0]
    north_vel = drift_kinematics[1]
    denominator = floe_weight + MOTION_STEP * WATER_DRAG
    new_east = (floe_weight * east_vel + MOTION_STEP * (force_x + external_drive[0] + WATER_DRAG * external_drive[2] + CORIOLIS * floe_weight * north_vel)) / denominator
    new_north = (floe_weight * north_vel + MOTION_STEP * (force_y + external_drive[1] + WATER_DRAG * external_drive[3] - CORIOLIS * floe_weight * east_vel)) / denominator
    return jnp.stack([new_east * water_mask, new_north * water_mask])

def reference(interface_conditions, level_warmth_profile, class_coverage_share, class_floe_depth, class_drift_depth, floe_drift_speed, internal_tension_tensor, external_drive, floe_weight, floe_pressure, holder_lookup, ground_tile_marker):
    patch_total = N_GX * N_GY
    tiles_row = HOLDER_PLACES // CAP
    blocks_of_grid = interface_conditions.reshape(POINT_QUANTITIES, N_GX, BPX, BS, N_GY, BPY, BS).transpose(1, 4, 2, 5, 0, 3, 6).reshape(GRID_BLOCK_COUNT, POINT_QUANTITIES, TILE_POINTS)
    target = holder_lookup[:, 0].reshape(patch_total, B)
    slot_covered = (1 - ground_tile_marker).reshape(patch_total, B)
    later = lax.broadcasted_iota(jnp.int32, (B, B), 1) < lax.broadcasted_iota(jnp.int32, (B, B), 0)
    matching = (target[:, :, None] == target[:, None, :]) & (slot_covered[:, None, :] == 1) & later[None]
    order_rank = lax.optimization_barrier(jnp.sum(matching.astype(jnp.int32), axis=2))
    tile_num = lax.broadcasted_iota(jnp.int32, (patch_total, B), 0)
    block_slot = (tile_num // tiles_row * tiles_row + target) * HOLDER_PLACES + tile_num % tiles_row * CAP + order_rank
    block_slot = jnp.where(slot_covered == 1, block_slot, HOLDER_POSITIONS).reshape(GRID_BLOCK_COUNT).astype(jnp.int32)
    quantities_each_position = jnp.zeros((HOLDER_POSITIONS, POINT_QUANTITIES, TILE_POINTS), jnp.float32).at[block_slot].set(blocks_of_grid, mode='drop')
    position_occupied = jnp.zeros((HOLDER_POSITIONS,), jnp.float32).at[block_slot].set(1.0, mode='drop')

    def by_holder(bundle):
        layer_temp, cat_area, cat_thick, cat_snow, owner_fields, owner_filled = bundle
        advanced_warmth, slot_fluxes = column_step(layer_temp, cat_area, cat_thick, cat_snow, owner_fields)
        kept = jnp.where(owner_filled[:, None, None, None] > 0.5, advanced_warmth, layer_temp)
        return (kept, slot_fluxes)
    renewed_heat_levels, outgoing_exchange_quantities = lax.map(by_holder, (level_warmth_profile.reshape(patch_total, HOLDER_PLACES, DEPTH_CLASSES, DRIFT_LEVELS + FROZEN_LEVELS, TILE_POINTS), class_coverage_share.reshape(patch_total, HOLDER_PLACES, DEPTH_CLASSES, TILE_POINTS), class_floe_depth.reshape(patch_total, HOLDER_PLACES, DEPTH_CLASSES, TILE_POINTS), class_drift_depth.reshape(patch_total, HOLDER_PLACES, DEPTH_CLASSES, TILE_POINTS), quantities_each_position.reshape(patch_total, HOLDER_PLACES, POINT_QUANTITIES, TILE_POINTS), position_occupied.reshape(patch_total, HOLDER_PLACES)))
    revised_level_warmth = renewed_heat_levels.reshape(HOLDER_POSITIONS, DEPTH_CLASSES, DRIFT_LEVELS + FROZEN_LEVELS, TILE_POINTS)
    flattened_fluxes = jnp.concatenate([outgoing_exchange_quantities.reshape(HOLDER_POSITIONS, 8, TILE_POINTS), jnp.zeros((1, 8, TILE_POINTS), jnp.float32)], axis=0)
    block_fluxes = jnp.take(flattened_fluxes, block_slot, axis=0)
    interface_exchanges = block_fluxes.reshape(N_GX, N_GY, BPX, BPY, 8, BS, BS).transpose(4, 0, 2, 5, 1, 3, 6).reshape(8, NX, NY)
    land_grid = ground_tile_marker.reshape(N_GX, N_GY, BPX, BPY).transpose(0, 2, 1, 3).reshape(N_GX * BPX, N_GY * BPY)
    water_mask = jnp.repeat(jnp.repeat(1.0 - land_grid.astype(jnp.float32), BS, axis=0), BS, axis=1)
    drift_kinematics = floe_drift_speed
    tension_components = internal_tension_tensor
    for subcycle in range(SUB):
        padded = jnp.pad(drift_kinematics, ((0, 0), (1, 1), (1, 1)))
        tension_components = update_stress(tension_components, floe_pressure, padded)
        force_x, force_y = stress_force(jnp.pad(tension_components, ((0, 0), (1, 1), (1, 1))))
        drift_kinematics = update_motion(drift_kinematics, force_x, force_y, floe_weight, external_drive, water_mask)
    return (revised_level_warmth, interface_exchanges, drift_kinematics, tension_components)
```

```python
import jax
import jax.numpy as jnp
from jax import lax
from jax.experimental import pallas as pl
from jax.experimental.pallas import tpu as pltpu
from jax.sharding import PartitionSpec as P

B = 16
CAP = 2
NSEND = 6
NBACK = 7
NF = 10
SUB = 4
NCAT = 5
NLAY = 10
NSNOW = 3
ROWS_OUT = NSEND * 8
ROWS_BACK = NBACK * 8

F32 = jnp.float32
VM = pltpu.VMEM
VSPEC = pl.BlockSpec(memory_space=pltpu.VMEM)
SSPEC = pl.BlockSpec(memory_space=pltpu.SMEM)


def lane_groups():
    return lax.broadcasted_iota(jnp.int32, (8, 128), 1) // 32


def swap_groups(rows, group):
    low = group < 2
    even = (group & 1) == 0
    v0, v1, v2, v3 = rows

    def roll(x, s):
        return pltpu.roll(x, s, 1)

    a0 = jnp.where(low, v0, roll(v2, 64))
    a2 = jnp.where(low, roll(v0, 64), v2)
    a1 = jnp.where(low, v1, roll(v3, 64))
    a3 = jnp.where(low, roll(v1, 64), v3)
    return (
        jnp.where(even, a0, roll(a1, 32)),
        jnp.where(even, roll(a0, 96), a1),
        jnp.where(even, a2, roll(a3, 32)),
        jnp.where(even, roll(a2, 96), a3),
    )


def block_slots(own, land, count):
    for o in range(B):
        count[o] = 0
    slots = []
    for b in range(B):
        o = own[b]
        r = count[o]
        slots.append(jnp.minimum(o * CAP + r, B * CAP - 1))
        count[o] = r + 1 - land[b]
    return slots


def pack_kernel(own, land, x, out, count):
    out[...] = jnp.zeros_like(out)
    slots = block_slots(own, land, count)
    group = lane_groups()
    for bx in range(4):
        def rows(f):
            return [x[f, pl.ds(32 * bx + q, 8, stride=4), :] for q in range(4)]

        visible, near_red, longwave = rows(3), rows(4), rows(5)
        fields = [
            rows(0),
            rows(1),
            rows(2),
            [0.25 * a + 0.45 * b + 0.3 * c for a, b, c in zip(visible, near_red, longwave)],
            rows(6),
            [1.0 / (1.0 + 2.0 * w) for w in rows(7)],
        ]
        blocks = [swap_groups(r, group) for r in fields]
        for by in range(4):
            b = 4 * bx + by

            @pl.when(land[b] == 0)
            def _():
                for f in range(NSEND):
                    out[pl.ds(pl.multiple_of(slots[b] * ROWS_OUT + f * 8, 8), 8), :] = blocks[f][by]


def pack(own, land, conditions):
    return pl.pallas_call(
        pack_kernel,
        out_shape=jax.ShapeDtypeStruct((B * CAP * ROWS_OUT, 128), F32),
        in_specs=[SSPEC, SSPEC, VSPEC],
        out_specs=VSPEC,
        scratch_shapes=[pltpu.SMEM((B,), jnp.int32)],
        name="pack",
    )(own, land, conditions)


def one_column(temps, share, floe, snow_depth, forcing, sig):
    ocean, air, source_top, top_resist = forcing
    h14 = floe * (1.0 / 14.0)
    h27 = floe * (2.0 / 7.0)
    h47 = floe * (4.0 / 7.0)
    m_snow = snow_depth * (2.0 / 3.0)
    half_snow = snow_depth * (0.5 / 0.9)
    g_snow = 0.9 / snow_depth
    g_top = 1.0 / (half_snow + top_resist)
    inv_cond = []
    mass = [m_snow] * NSNOW
    for j in range(NLAY - NSNOW):
        t = temps[NSNOW + j]
        inv_cond.append(1.0 / (2.0 + sig[j] / (t - 0.5)))
        mass.append(h27 + h47 * (sig[j] / (t * t + 0.1)))
    cond = [g_snow, g_snow, 1.0 / (half_snow + h14 * inv_cond[0])]
    for j in range(NLAY - NSNOW - 1):
        cond.append(1.0 / (h14 * (inv_cond[j] + inv_cond[j + 1])))
    g_bot = 1.0 / (h14 * inv_cond[-1])
    ratios = []
    values = []
    u = mass[0] + g_top
    held = mass[0] * temps[0]
    y = held + g_top * air + source_top
    for l in range(NLAY):
        below = cond[l] if l < NLAY - 1 else g_bot
        pivot = 1.0 / (u + below)
        ratio = below * pivot
        if l < NLAY - 1:
            ratios.append(ratio)
            values.append(y * pivot)
            u = mass[l + 1] + ratio * u
            mt = mass[l + 1] * temps[l + 1]
            held = held + mt
            y = mt + ratio * y
        else:
            last = y * pivot + ratio * ocean
    solved = [last]
    for l in range(NLAY - 2, -1, -1):
        solved.insert(0, values[l] + ratios[l] * solved[0])
    bottom = share * (g_bot * (last - ocean))
    top = share * (g_top * (air - solved[0]))
    light = share * jnp.exp(-5.0 * snow_depth - 1.5 * floe)
    return solved, (
        bottom,
        top,
        light,
        share * solved[0],
        share * snow_depth,
        share * floe,
        share * held,
        share,
    )


def column_kernel(warm, share, floe, drift, recv, new_warm, flux):
    half = pl.program_id(1)

    def tile(k, carry):
        lanes = pl.ds(pl.multiple_of(k * 128, 128), 128)
        kk = half * 4 + k

        def field(f):
            return recv[pl.ds(f * 8 + kk, 8, stride=ROWS_OUT), :]

        ocean, salinity, air, source_top, snowfall, top_resist = [field(f) for f in range(NSEND)]
        filled = salinity > 0.25
        sig = [salinity * (0.02 + 0.01 * j) for j in range(NLAY - NSNOW)]
        snow_add = 0.3 * snowfall
        sums = None
        for c in range(NCAT):
            temps = [warm[c, l, :, lanes] for l in range(NLAY)]
            solved, terms = one_column(
                temps,
                share[c, :, lanes],
                floe[c, :, lanes],
                drift[c, :, lanes] + snow_add,
                (ocean, air, source_top, top_resist),
                sig,
            )
            for l in range(NLAY):
                new_warm[c, l, :, lanes] = jnp.where(filled, solved[l], temps[l])
            sums = terms if sums is None else tuple(a + b for a, b in zip(sums, terms))
        bottom, top, light, surface, snow, thick, held, total = sums
        back = (
            bottom,
            top,
            light,
            surface,
            snow,
            thick - 0.05 * bottom,
            0.05 * (held + top - bottom + source_top * total),
        )
        for f in range(NBACK):
            flux[pl.ds(f * 8 + kk, 8, stride=ROWS_BACK), :] = back[f]
        return carry

    lax.fori_loop(0, 4, tile, 0)


def columns(warm, share, floe, drift, recv):
    cls = pl.BlockSpec((NCAT, 8, 512), lambda g, h: (0, g, h))
    col = pl.BlockSpec((NCAT, NLAY, 8, 512), lambda g, h: (0, 0, g, h))
    return pl.pallas_call(
        column_kernel,
        grid=(4, 2),
        out_shape=(
            jax.ShapeDtypeStruct((NCAT, NLAY, 32, 1024), F32),
            jax.ShapeDtypeStruct((B * CAP * ROWS_BACK, 128), F32),
        ),
        in_specs=[col, cls, cls, cls, pl.BlockSpec((8 * ROWS_OUT, 128), lambda g, h: (g, 0))],
        out_specs=(col, pl.BlockSpec((8 * ROWS_BACK, 128), lambda g, h: (g, 0))),
        name="columns",
    )(warm, share, floe, drift, recv)


def unpack_kernel(own, land, back, salinity, visible, out, count):
    slots = block_slots(own, land, count)
    group = lane_groups()
    for bx in range(4):
        rows = []
        for f in range(NBACK):
            blocks = []
            for by in range(4):
                b = 4 * bx + by
                v = back[pl.ds(pl.multiple_of(slots[b] * ROWS_BACK + f * 8, 8), 8), :]
                blocks.append(jnp.where(land[b] == 0, v, 0.0))
            rows.append(swap_groups(blocks, group))
        for q in range(4):
            at = pl.ds(32 * bx + q, 8, stride=4)
            sal = salinity[0, at, :]
            vis = visible[0, at, :]
            for f in range(NBACK):
                v = rows[f][q]
                out[f, at, :] = (0.7 * vis) * v if f == 2 else v
            out[7, at, :] = (-0.05 * sal) * rows[0][q]


def unpack(own, land, back, conditions):
    return pl.pallas_call(
        unpack_kernel,
        grid=(1,),
        out_shape=jax.ShapeDtypeStruct((8, 128, 128), F32),
        in_specs=[
            SSPEC,
            SSPEC,
            pl.BlockSpec((B * CAP * ROWS_BACK, 128), lambda i: (0, 0)),
            pl.BlockSpec((1, 128, 128), lambda i: (1, 0, 0)),
            pl.BlockSpec((1, 128, 128), lambda i: (3, 0, 0)),
        ],
        out_specs=pl.BlockSpec((8, 128, 128), lambda i: (0, 0, 0)),
        scratch_shapes=[pltpu.SMEM((B,), jnp.int32)],
        name="unpack",
    )(own, land, back, conditions, conditions)


def prepare_kernel(land, vel, stress, drive, weight, pressure, coef, up, down):
    group = lax.broadcasted_iota(jnp.int32, (32, 128), 1) // 32
    for bx in range(4):
        at = pl.ds(32 * bx, 32)
        water = jnp.zeros((32, 128), F32)
        for by in range(4):
            water = jnp.where(group == by, (1 - land[4 * bx + by]).astype(F32), water)
        w = weight[at, :]
        scale = water / (w + 0.5)
        beta = 0.5 * scale
        coef[0, at, :] = pressure[at, :] * (1.0 / 3.0)
        coef[1, at, :] = scale * w
        coef[2, at, :] = 0.25 * beta
        coef[3, at, :] = beta * (drive[0, at, :] + drive[2, at, :])
        coef[4, at, :] = beta * (drive[1, at, :] + drive[3, at, :])
    for rows, dst in ((pl.ds(0, 8), up), (pl.ds(120, 8), down)):
        dst[0:2] = vel[:, rows, :]
        dst[2:5] = stress[:, rows, :]
        dst[5:10] = coef[:, rows, :]


def prepare(land, vel, stress, drive, weight, pressure):
    edge = jax.ShapeDtypeStruct((NF, 8, 128), F32)
    return pl.pallas_call(
        prepare_kernel,
        out_shape=(jax.ShapeDtypeStruct((5, 128, 128), F32), edge, edge),
        in_specs=[SSPEC] + [VSPEC] * 5,
        out_specs=(VSPEC, VSPEC, VSPEC),
        name="prepare",
    )(land, vel, stress, drive, weight, pressure)


NPACK = 12


def field_tile(f, t, vel, stress, coef, top, bottom):
    if t == 0:
        return top[f]
    if t == 17:
        return bottom[f]
    rows = slice(8 * (t - 1), 8 * t)
    if f < 2:
        return vel[f, rows, :]
    if f < 5:
        return stress[f - 2, rows, :]
    return coef[f - 5, rows, :]


def edges_kernel(vel, stress, coef, top, bottom, left, right):
    piece = lax.broadcasted_iota(jnp.int32, (8, 128), 1) // 8
    for v in range(NPACK):
        to_left = jnp.zeros((8, 128), F32)
        to_right = jnp.zeros((8, 128), F32)
        for i in range(16):
            n = 16 * v + i
            if n >= NF * 18:
                break
            x = field_tile(n // 18, n % 18, vel, stress, coef, top, bottom)
            xl = pltpu.roll(x, 8 * i, 1) if i else x
            xr = pltpu.roll(x, (8 * i + 8) % 128, 1) if i < 15 else x
            to_left = jnp.where(piece == i, xl, to_left)
            to_right = jnp.where(piece == i, xr, to_right)
        left[v] = to_left
        right[v] = to_right


def edges(vel, stress, coef, top, bottom):
    side = jax.ShapeDtypeStruct((NPACK, 8, 128), F32)
    return pl.pallas_call(
        edges_kernel,
        out_shape=(side, side),
        in_specs=[VSPEC] * 5,
        out_specs=(VSPEC, VSPEC),
        name="edges",
    )(vel, stress, coef, top, bottom)


GUARD = 8


def evp_kernel(vel, stress, coef, top, bottom, left, right, vel_out, stress_out, ext):
    lane = lax.broadcasted_iota(jnp.int32, (8, 128), 1)
    for f in range(NF):
        ext[f, 0:8, :] = jnp.zeros((8, 256), F32)
        ext[f, 152:160, :] = jnp.zeros((8, 256), F32)
        for t in range(18):
            n = f * 18 + t
            v, i = divmod(n, 16)
            rows = slice(GUARD + 8 * t, GUARD + 8 * t + 8)
            ext[f, rows, 0:128] = field_tile(f, t, vel, stress, coef, top, bottom)
            from_right = pltpu.roll(right[v], (128 - 8 * i) % 128, 1) if i else right[v]
            from_left = pltpu.roll(left[v], (120 - 8 * i) % 128, 1) if i < 15 else left[v]
            ext[f, rows, 128:256] = jnp.where(
                lane < 8, from_right, jnp.where(lane >= 120, from_left, 0.0)
            )

    def before(x):
        return pltpu.roll(x, 1, 1)

    def after(x):
        return pltpu.roll(x, 255, 1)

    def subcycle(step, carry):
        for t in range(18):
            r = GUARD + 8 * t
            here = pl.ds(r, 8)
            east = ext[0, here, :]
            north = ext[1, here, :]
            a = ext[0, pl.ds(r + 1, 8), :] - ext[0, pl.ds(r - 1, 8), :]
            d = ext[1, pl.ds(r + 1, 8), :] - ext[1, pl.ds(r - 1, 8), :]
            b = after(north) - before(north)
            c = after(east) - before(east)
            plus = a + b
            minus = a - b
            shear = c + d
            square = 0.25 * (plus * plus) + 0.0625 * (minus * minus + shear * shear) + 0.04
            p3 = ext[5, here, :]
            k = p3 * lax.rsqrt(square)
            ext[2, here, :] = (2.0 / 3.0) * ext[2, here, :] + (0.5 * k) * plus - p3
            ext[3, here, :] = (2.0 / 3.0) * ext[3, here, :] + (0.125 * k) * minus
            ext[4, here, :] = (2.0 / 3.0) * ext[4, here, :] + (0.0625 * k) * shear
        for t in range(18):
            r = GUARD + 8 * t
            here = pl.ds(r, 8)
            down = pl.ds(r + 1, 8)
            up = pl.ds(r - 1, 8)
            s2 = ext[4, here, :]
            differ = ext[2, here, :] - ext[3, here, :]
            force_x = (ext[2, down, :] + ext[3, down, :]) - (ext[2, up, :] + ext[3, up, :])
            force_x = force_x + 2.0 * (after(s2) - before(s2))
            force_y = after(differ) - before(differ)
            force_y = force_y + 2.0 * (ext[4, down, :] - ext[4, up, :])
            alpha = ext[6, here, :]
            beta = ext[7, here, :]
            east = ext[0, here, :]
            north = ext[1, here, :]
            ext[0, here, :] = alpha * (east + 0.15 * north) + beta * force_x + ext[8, here, :]
            ext[1, here, :] = alpha * (north - 0.15 * east) + beta * force_y + ext[9, here, :]
        return carry

    lax.fori_loop(0, SUB, subcycle, 0)
    inner = slice(GUARD + 8, GUARD + 136)
    for f in range(2):
        vel_out[f] = ext[f, inner, 0:128]
    for f in range(3):
        stress_out[f] = ext[2 + f, inner, 0:128]


def evp(vel, stress, coef, top, bottom, left, right):
    return pl.pallas_call(
        evp_kernel,
        out_shape=(
            jax.ShapeDtypeStruct((2, 128, 128), F32),
            jax.ShapeDtypeStruct((3, 128, 128), F32),
        ),
        in_specs=[VSPEC] * 7,
        out_specs=(VSPEC, VSPEC),
        scratch_shapes=[pltpu.VMEM((NF, 160, 256), F32)],
        name="evp",
    )(vel, stress, coef, top, bottom, left, right)


def exchange(axis, to_lower, to_upper):
    peers = lax.axis_size(axis)
    up = [(i, i + 1) for i in range(peers - 1)]
    down = [(i + 1, i) for i in range(peers - 1)]
    return lax.ppermute(to_upper, axis, up), lax.ppermute(to_lower, axis, down)


def swap(payload, rows):
    n = lax.axis_size("gy")
    out = lax.all_to_all(
        payload.reshape(n, CAP * rows, 128), "gy", split_axis=0, concat_axis=0, tiled=True
    )
    return out.reshape(n * CAP * rows, 128)


def local(
    conditions,
    warmth,
    share,
    floe,
    drift,
    velocity,
    stress,
    drive,
    weight,
    pressure,
    holder,
    land,
):
    own = holder.reshape(B)
    recv = swap(pack(own, land, conditions), ROWS_OUT)

    coef, first_rows, last_rows = prepare(land, velocity, stress, drive, weight, pressure)
    top, bottom = exchange("gx", first_rows, last_rows)
    to_left, to_right = edges(velocity, stress, coef, top, bottom)
    left, right = exchange("gy", to_left, to_right)

    new_warm, flux = columns(
        warmth.transpose(1, 2, 0, 3),
        share.transpose(1, 0, 2),
        floe.transpose(1, 0, 2),
        drift.transpose(1, 0, 2),
        recv,
    )
    back = swap(flux, ROWS_BACK)
    velocity_new, stress_new = evp(velocity, stress, coef, top, bottom, left, right)
    exchanges = unpack(own, land, back, conditions)
    return (new_warm.transpose(2, 0, 1, 3), exchanges, velocity_new, stress_new)


def solution(mesh):
    return jax.shard_map(
        local,
        mesh=mesh,
        in_specs=(
            P(None, "gx", "gy"),
            P(("gx", "gy"), None, None, None),
            P(("gx", "gy"), None, None),
            P(("gx", "gy"), None, None),
            P(("gx", "gy"), None, None),
            P(None, "gx", "gy"),
            P(None, "gx", "gy"),
            P(None, "gx", "gy"),
            P("gx", "gy"),
            P("gx", "gy"),
            P(("gx", "gy"), None),
            P(("gx", "gy")),
        ),
        out_specs=(
            P(("gx", "gy"), None, None, None),
            P(None, "gx", "gy"),
            P(None, "gx", "gy"),
            P(None, "gx", "gy"),
        ),
        check_vma=False,
    )
```

```python
import jax
import jax.numpy as jnp
from jax import lax
from jax.experimental import pallas as pl
from jax.experimental.pallas import tpu as pltpu
from jax.sharding import PartitionSpec as P

B = 16
CAP = 2
NSEND = 6
NBACK = 7
NF = 10
SUB = 4
NCAT = 5
NLAY = 10
NSNOW = 3
ROWS_OUT = NSEND * 8
ROWS_BACK = NBACK * 8

F32 = jnp.float32
VM = pltpu.VMEM
VSPEC = pl.BlockSpec(memory_space=pltpu.VMEM)
SSPEC = pl.BlockSpec(memory_space=pltpu.SMEM)


def vmem(*arrays):
    out = [pltpu.with_memory_space_constraint(a, pltpu.VMEM) for a in arrays]
    return out if len(out) > 1 else out[0]


def lane_groups():
    return lax.broadcasted_iota(jnp.int32, (8, 128), 1) // 32


def swap_groups(rows, group):
    low = group < 2
    even = (group & 1) == 0
    v0, v1, v2, v3 = rows

    def roll(x, s):
        return pltpu.roll(x, s, 1)

    a0 = jnp.where(low, v0, roll(v2, 64))
    a2 = jnp.where(low, roll(v0, 64), v2)
    a1 = jnp.where(low, v1, roll(v3, 64))
    a3 = jnp.where(low, roll(v1, 64), v3)
    return (
        jnp.where(even, a0, roll(a1, 32)),
        jnp.where(even, roll(a0, 96), a1),
        jnp.where(even, a2, roll(a3, 32)),
        jnp.where(even, roll(a2, 96), a3),
    )


def block_slots(own, land, count):
    for o in range(B):
        count[o] = 0
    slots = []
    for b in range(B):
        o = own[b]
        r = count[o]
        slots.append(jnp.minimum(o * CAP + r, B * CAP - 1))
        count[o] = r + 1 - land[b]
    return slots


def pack_kernel(own, land, x, out, count):
    out[...] = jnp.zeros_like(out)
    slots = block_slots(own, land, count)
    group = lane_groups()
    for bx in range(4):
        def rows(f):
            return [x[f, pl.ds(32 * bx + q, 8, stride=4), :] for q in range(4)]

        visible, near_red, longwave = rows(3), rows(4), rows(5)
        fields = [
            rows(0),
            rows(1),
            rows(2),
            [0.25 * a + 0.45 * b + 0.3 * c for a, b, c in zip(visible, near_red, longwave)],
            rows(6),
            [1.0 / (1.0 + 2.0 * w) for w in rows(7)],
        ]
        blocks = [swap_groups(r, group) for r in fields]
        for by in range(4):
            b = 4 * bx + by

            @pl.when(land[b] == 0)
            def _():
                for f in range(NSEND):
                    out[pl.ds(pl.multiple_of(slots[b] * ROWS_OUT + f * 8, 8), 8), :] = blocks[f][by]


def pack(own, land, conditions):
    return pl.pallas_call(
        pack_kernel,
        out_shape=pltpu.VMEM((B * CAP * ROWS_OUT, 128), F32),
        in_specs=[SSPEC, SSPEC, VSPEC],
        out_specs=VSPEC,
        scratch_shapes=[pltpu.SMEM((B,), jnp.int32)],
        name="pack",
    )(own, land, conditions)


def one_column(temps, share, floe, snow_depth, forcing, sig):
    ocean, air, source_top, top_resist = forcing
    h14 = floe * (1.0 / 14.0)
    h27 = floe * (2.0 / 7.0)
    h47 = floe * (4.0 / 7.0)
    m_snow = snow_depth * (2.0 / 3.0)
    half_snow = snow_depth * (0.5 / 0.9)
    g_snow = 0.9 / snow_depth
    g_top = 1.0 / (half_snow + top_resist)
    inv_cond = []
    mass = [m_snow] * NSNOW
    for j in range(NLAY - NSNOW):
        t = temps[NSNOW + j]
        inv_cond.append(1.0 / (2.0 + sig[j] / (t - 0.5)))
        mass.append(h27 + h47 * (sig[j] / (t * t + 0.1)))
    cond = [g_snow, g_snow, 1.0 / (half_snow + h14 * inv_cond[0])]
    for j in range(NLAY - NSNOW - 1):
        cond.append(1.0 / (h14 * (inv_cond[j] + inv_cond[j + 1])))
    g_bot = 1.0 / (h14 * inv_cond[-1])
    ratios = []
    values = []
    u = mass[0] + g_top
    held = mass[0] * temps[0]
    y = held + g_top * air + source_top
    for l in range(NLAY):
        below = cond[l] if l < NLAY - 1 else g_bot
        pivot = 1.0 / (u + below)
        ratio = below * pivot
        if l < NLAY - 1:
            ratios.append(ratio)
            values.append(y * pivot)
            u = mass[l + 1] + ratio * u
            mt = mass[l + 1] * temps[l + 1]
            held = held + mt
            y = mt + ratio * y
        else:
            last = y * pivot + ratio * ocean
    solved = [last]
    for l in range(NLAY - 2, -1, -1):
        solved.insert(0, values[l] + ratios[l] * solved[0])
    bottom = share * (g_bot * (last - ocean))
    top = share * (g_top * (air - solved[0]))
    light = share * jnp.exp(-5.0 * snow_depth - 1.5 * floe)
    return solved, (
        bottom,
        top,
        light,
        share * solved[0],
        share * snow_depth,
        share * floe,
        share * held,
        share,
    )


def column_kernel(warm, share, floe, drift, recv, new_warm, flux):
    first = pl.program_id(0) * 8
    half = pl.program_id(1)

    def tile(k, carry):
        lanes = pl.ds(pl.multiple_of(k * 128, 128), 128)
        kk = half * 4 + k

        def field(f):
            return recv[pl.ds(first * ROWS_OUT + f * 8 + kk, 8, stride=ROWS_OUT), :]

        ocean, salinity, air, source_top, snowfall, top_resist = [field(f) for f in range(NSEND)]
        filled = salinity > 0.25
        sig = [salinity * (0.02 + 0.01 * j) for j in range(NLAY - NSNOW)]
        snow_add = 0.3 * snowfall
        sums = None
        for c in range(NCAT):
            temps = [warm[c, l, :, lanes] for l in range(NLAY)]
            solved, terms = one_column(
                temps,
                share[c, :, lanes],
                floe[c, :, lanes],
                drift[c, :, lanes] + snow_add,
                (ocean, air, source_top, top_resist),
                sig,
            )
            for l in range(NLAY):
                new_warm[c, l, :, lanes] = jnp.where(filled, solved[l], temps[l])
            sums = terms if sums is None else tuple(a + b for a, b in zip(sums, terms))
        bottom, top, light, surface, snow, thick, held, total = sums
        back = (
            bottom,
            top,
            light,
            surface,
            snow,
            thick - 0.05 * bottom,
            0.05 * (held + top - bottom + source_top * total),
        )
        for f in range(NBACK):
            flux[pl.ds(first * ROWS_BACK + f * 8 + kk, 8, stride=ROWS_BACK), :] = back[f]
        return carry

    lax.fori_loop(0, 4, tile, 0)


def columns(warm, share, floe, drift, recv):
    cls = pl.BlockSpec((NCAT, 8, 512), lambda g, h: (0, g, h))
    col = pl.BlockSpec((NCAT, NLAY, 8, 512), lambda g, h: (0, 0, g, h))
    return pl.pallas_call(
        column_kernel,
        grid=(4, 2),
        out_shape=(
            jax.ShapeDtypeStruct((NCAT, NLAY, 32, 1024), F32),
            pltpu.VMEM((B * CAP * ROWS_BACK, 128), F32),
        ),
        in_specs=[col, cls, cls, cls, VSPEC],
        out_specs=(col, VSPEC),
        name="columns",
    )(warm, share, floe, drift, vmem(recv))


def unpack_kernel(own, land, back, salinity, visible, out, count):
    slots = block_slots(own, land, count)
    group = lane_groups()
    for bx in range(4):
        rows = []
        for f in range(NBACK):
            blocks = []
            for by in range(4):
                b = 4 * bx + by
                v = back[pl.ds(pl.multiple_of(slots[b] * ROWS_BACK + f * 8, 8), 8), :]
                blocks.append(jnp.where(land[b] == 0, v, 0.0))
            rows.append(swap_groups(blocks, group))
        for q in range(4):
            at = pl.ds(32 * bx + q, 8, stride=4)
            sal = salinity[0, at, :]
            vis = visible[0, at, :]
            for f in range(NBACK):
                v = rows[f][q]
                out[f, at, :] = (0.7 * vis) * v if f == 2 else v
            out[7, at, :] = (-0.05 * sal) * rows[0][q]


def unpack(own, land, back, conditions):
    return pl.pallas_call(
        unpack_kernel,
        grid=(1,),
        out_shape=jax.ShapeDtypeStruct((8, 128, 128), F32),
        in_specs=[
            SSPEC,
            SSPEC,
            VSPEC,
            pl.BlockSpec((1, 128, 128), lambda i: (1, 0, 0)),
            pl.BlockSpec((1, 128, 128), lambda i: (3, 0, 0)),
        ],
        out_specs=pl.BlockSpec((8, 128, 128), lambda i: (0, 0, 0)),
        scratch_shapes=[pltpu.SMEM((B,), jnp.int32)],
        name="unpack",
    )(own, land, vmem(back), conditions, conditions)


def prepare_kernel(land, vel, stress, drive, weight, pressure, fields, up, down):
    group = lax.broadcasted_iota(jnp.int32, (32, 128), 1) // 32
    fields[0:2] = vel[...]
    fields[2:5] = stress[...]
    for bx in range(4):
        at = pl.ds(32 * bx, 32)
        water = jnp.zeros((32, 128), F32)
        for by in range(4):
            water = jnp.where(group == by, (1 - land[4 * bx + by]).astype(F32), water)
        w = weight[at, :]
        scale = water / (w + 0.5)
        beta = 0.5 * scale
        fields[5, at, :] = pressure[at, :] * (1.0 / 3.0)
        fields[6, at, :] = scale * w
        fields[7, at, :] = 0.25 * beta
        fields[8, at, :] = beta * (drive[0, at, :] + drive[2, at, :])
        fields[9, at, :] = beta * (drive[1, at, :] + drive[3, at, :])
    up[...] = fields[:, 0:8, :]
    down[...] = fields[:, 120:128, :]


def prepare(land, vel, stress, drive, weight, pressure):
    edge = pltpu.VMEM((NF, 8, 128), F32)
    return pl.pallas_call(
        prepare_kernel,
        out_shape=(pltpu.VMEM((NF, 128, 128), F32), edge, edge),
        in_specs=[SSPEC] + [VSPEC] * 5,
        out_specs=(VSPEC, VSPEC, VSPEC),
        name="prepare",
    )(land, vel, stress, drive, weight, pressure)


NPACK = 12


def field_tile(f, t, fields, top, bottom):
    if t == 0:
        return top[f]
    if t == 17:
        return bottom[f]
    return fields[f, 8 * (t - 1) : 8 * t, :]


def edges_kernel(fields, top, bottom, left, right):
    piece = lax.broadcasted_iota(jnp.int32, (8, 128), 1) // 8
    for v in range(NPACK):
        to_left = jnp.zeros((8, 128), F32)
        to_right = jnp.zeros((8, 128), F32)
        for i in range(16):
            n = 16 * v + i
            if n >= NF * 18:
                break
            x = field_tile(n // 18, n % 18, fields, top, bottom)
            xl = pltpu.roll(x, 8 * i, 1) if i else x
            xr = pltpu.roll(x, (8 * i + 8) % 128, 1) if i < 15 else x
            to_left = jnp.where(piece == i, xl, to_left)
            to_right = jnp.where(piece == i, xr, to_right)
        left[v] = to_left
        right[v] = to_right


def edges(fields, top, bottom):
    side = pltpu.VMEM((NPACK, 8, 128), F32)
    return pl.pallas_call(
        edges_kernel,
        out_shape=(side, side),
        in_specs=[VSPEC] * 3,
        out_specs=(VSPEC, VSPEC),
        name="edges",
    )(*vmem(fields, top, bottom))


GUARD = 8


def evp_kernel(fields, top, bottom, left, right, vel_out, stress_out, ext):
    lane = lax.broadcasted_iota(jnp.int32, (8, 128), 1)
    for f in range(NF):
        ext[f, 0:8, :] = jnp.zeros((8, 256), F32)
        ext[f, 152:160, :] = jnp.zeros((8, 256), F32)
        for t in range(18):
            n = f * 18 + t
            v, i = divmod(n, 16)
            rows = slice(GUARD + 8 * t, GUARD + 8 * t + 8)
            ext[f, rows, 0:128] = field_tile(f, t, fields, top, bottom)
            from_right = pltpu.roll(right[v], (128 - 8 * i) % 128, 1) if i else right[v]
            from_left = pltpu.roll(left[v], (120 - 8 * i) % 128, 1) if i < 15 else left[v]
            ext[f, rows, 128:256] = jnp.where(
                lane < 8, from_right, jnp.where(lane >= 120, from_left, 0.0)
            )

    def before(x):
        return pltpu.roll(x, 1, 1)

    def after(x):
        return pltpu.roll(x, 255, 1)

    def subcycle(step, carry):
        for t in range(18):
            r = GUARD + 8 * t
            here = pl.ds(r, 8)
            east = ext[0, here, :]
            north = ext[1, here, :]
            a = ext[0, pl.ds(r + 1, 8), :] - ext[0, pl.ds(r - 1, 8), :]
            d = ext[1, pl.ds(r + 1, 8), :] - ext[1, pl.ds(r - 1, 8), :]
            b = after(north) - before(north)
            c = after(east) - before(east)
            plus = a + b
            minus = a - b
            shear = c + d
            square = 0.25 * (plus * plus) + 0.0625 * (minus * minus + shear * shear) + 0.04
            p3 = ext[5, here, :]
            k = p3 * lax.rsqrt(square)
            ext[2, here, :] = (2.0 / 3.0) * ext[2, here, :] + (0.5 * k) * plus - p3
            ext[3, here, :] = (2.0 / 3.0) * ext[3, here, :] + (0.125 * k) * minus
            ext[4, here, :] = (2.0 / 3.0) * ext[4, here, :] + (0.0625 * k) * shear
        for t in range(18):
            r = GUARD + 8 * t
            here = pl.ds(r, 8)
            down = pl.ds(r + 1, 8)
            up = pl.ds(r - 1, 8)
            s2 = ext[4, here, :]
            differ = ext[2, here, :] - ext[3, here, :]
            force_x = (ext[2, down, :] + ext[3, down, :]) - (ext[2, up, :] + ext[3, up, :])
            force_x = force_x + 2.0 * (after(s2) - before(s2))
            force_y = after(differ) - before(differ)
            force_y = force_y + 2.0 * (ext[4, down, :] - ext[4, up, :])
            alpha = ext[6, here, :]
            beta = ext[7, here, :]
            east = ext[0, here, :]
            north = ext[1, here, :]
            ext[0, here, :] = alpha * (east + 0.15 * north) + beta * force_x + ext[8, here, :]
            ext[1, here, :] = alpha * (north - 0.15 * east) + beta * force_y + ext[9, here, :]
        return carry

    lax.fori_loop(0, SUB, subcycle, 0)
    inner = slice(GUARD + 8, GUARD + 136)
    for f in range(2):
        vel_out[f] = ext[f, inner, 0:128]
    for f in range(3):
        stress_out[f] = ext[2 + f, inner, 0:128]


def evp(fields, top, bottom, left, right):
    return pl.pallas_call(
        evp_kernel,
        out_shape=(
            jax.ShapeDtypeStruct((2, 128, 128), F32),
            jax.ShapeDtypeStruct((3, 128, 128), F32),
        ),
        in_specs=[VSPEC] * 5,
        out_specs=(VSPEC, VSPEC),
        scratch_shapes=[pltpu.VMEM((NF, 160, 256), F32)],
        name="evp",
    )(*vmem(fields, top, bottom, left, right))


def exchange(axis, to_lower, to_upper):
    peers = lax.axis_size(axis)
    up = [(i, i + 1) for i in range(peers - 1)]
    down = [(i + 1, i) for i in range(peers - 1)]
    return lax.ppermute(to_upper, axis, up), lax.ppermute(to_lower, axis, down)


def swap(payload, rows):
    n = lax.axis_size("gy")
    out = lax.all_to_all(
        payload.reshape(n, CAP * rows, 128), "gy", split_axis=0, concat_axis=0, tiled=True
    )
    return out.reshape(n * CAP * rows, 128)


def local(
    conditions,
    warmth,
    share,
    floe,
    drift,
    velocity,
    stress,
    drive,
    weight,
    pressure,
    holder,
    land,
):
    own = holder.reshape(B)
    recv = swap(pack(own, land, conditions), ROWS_OUT)

    fields, first_rows, last_rows = prepare(land, velocity, stress, drive, weight, pressure)
    top, bottom = exchange("gx", first_rows, last_rows)
    to_left, to_right = edges(fields, top, bottom)
    warmth, to_left, to_right = lax.optimization_barrier((warmth, to_left, to_right))
    new_warm, flux = columns(
        warmth.transpose(1, 2, 0, 3),
        share.transpose(1, 0, 2),
        floe.transpose(1, 0, 2),
        drift.transpose(1, 0, 2),
        recv,
    )
    back = swap(flux, ROWS_BACK)
    left, right = exchange("gy", to_left, to_right)
    velocity_new, stress_new = evp(fields, top, bottom, left, right)
    exchanges = unpack(own, land, back, conditions)
    return (new_warm.transpose(2, 0, 1, 3), exchanges, velocity_new, stress_new)


def solution(mesh):
    return jax.shard_map(
        local,
        mesh=mesh,
        in_specs=(
            P(None, "gx", "gy"),
            P(("gx", "gy"), None, None, None),
            P(("gx", "gy"), None, None),
            P(("gx", "gy"), None, None),
            P(("gx", "gy"), None, None),
            P(None, "gx", "gy"),
            P(None, "gx", "gy"),
            P(None, "gx", "gy"),
            P("gx", "gy"),
            P("gx", "gy"),
            P(("gx", "gy"), None),
            P(("gx", "gy")),
        ),
        out_specs=(
            P(("gx", "gy"), None, None, None),
            P(None, "gx", "gy"),
            P(None, "gx", "gy"),
            P(None, "gx", "gy"),
        ),
        check_vma=False,
    )
```

```python
import jax
import jax.numpy as jnp
from jax import lax
from jax.experimental import pallas as pl
from jax.experimental.pallas import tpu as pltpu
from jax.sharding import PartitionSpec as P


B = 16
CAP = 2
NSEND = 6
NBACK = 7
NF = 10
SUB = 4
NCAT = 5
NLAY = 10
NSNOW = 3
ROWS_OUT = NSEND * 8
ROWS_BACK = NBACK * 8

F32 = jnp.float32
LOG2E = 1.4426950408889634
VSPEC = pl.BlockSpec(memory_space=pltpu.VMEM)
SSPEC = pl.BlockSpec(memory_space=pltpu.SMEM)


def vmem(*arrays):
    out = [pltpu.with_memory_space_constraint(a, pltpu.VMEM) for a in arrays]
    return out if len(out) > 1 else out[0]


def lane_groups():
    return lax.broadcasted_iota(jnp.int32, (8, 128), 1) // 32


def swap_groups(rows, group):
    low = group < 2
    even = (group & 1) == 0
    v0, v1, v2, v3 = rows

    def roll(x, s):
        return pltpu.roll(x, s, 1)

    a0 = jnp.where(low, v0, roll(v2, 64))
    a2 = jnp.where(low, roll(v0, 64), v2)
    a1 = jnp.where(low, v1, roll(v3, 64))
    a3 = jnp.where(low, roll(v1, 64), v3)
    return (
        jnp.where(even, a0, roll(a1, 32)),
        jnp.where(even, roll(a0, 96), a1),
        jnp.where(even, a2, roll(a3, 32)),
        jnp.where(even, roll(a2, 96), a3),
    )


def block_slots(own, land, count, blocks):
    slots = []
    for b in blocks:
        o = own[b]
        r = count[o]
        slots.append(jnp.minimum(o * CAP + r, B * CAP - 1))
        count[o] = r + 1 - land[b]
    return slots


def start_count(count):
    for o in range(B):
        count[o] = 0


def pack_kernel(own, land, x, out, kept, count):
    out[...] = jnp.zeros_like(out)
    kept[0] = 0.7 * x[3]
    kept[1] = -0.05 * x[1]
    start_count(count)
    slots = block_slots(own, land, count, range(B))
    group = lane_groups()
    for bx in range(4):

        def rows(f):
            return [x[f, pl.ds(32 * bx + q, 8, stride=4), :] for q in range(4)]

        visible, near_red, longwave = rows(3), rows(4), rows(5)
        fields = [
            rows(0),
            rows(1),
            rows(2),
            [0.25 * a + 0.45 * b + 0.3 * c for a, b, c in zip(visible, near_red, longwave)],
            rows(6),
            [1.0 / (1.0 + 2.0 * w) for w in rows(7)],
        ]
        blocks = [swap_groups(r, group) for r in fields]
        for by in range(4):
            b = 4 * bx + by

            @pl.when(land[b] == 0)
            def _():
                for f in range(NSEND):
                    out[pl.ds(pl.multiple_of(slots[b] * ROWS_OUT + f * 8, 8), 8), :] = blocks[f][by]


def pack(own, land, conditions):
    return pl.pallas_call(
        pack_kernel,
        out_shape=(pltpu.VMEM((B * CAP * ROWS_OUT, 128), F32), pltpu.VMEM((2, 128, 128), F32)),
        in_specs=[SSPEC, SSPEC, VSPEC],
        out_specs=(VSPEC, VSPEC),
        scratch_shapes=[pltpu.SMEM((B,), jnp.int32)],
        name="pack",
    )(own, land, conditions)


def one_column(temps, share, floe, snow_depth, forcing, sig):
    ocean, air, source_top, top_resist = forcing
    h14 = floe * (1.0 / 14.0)
    h27 = floe * (2.0 / 7.0)
    h47 = floe * (4.0 / 7.0)
    m_snow = snow_depth * (2.0 / 3.0)
    half_snow = snow_depth * (0.5 / 0.9)
    g_snow = 0.9 / snow_depth
    g_top = 1.0 / (half_snow + top_resist)
    inv_cond = []
    mass = [m_snow] * NSNOW
    for j in range(NLAY - NSNOW):
        t = temps[NSNOW + j]
        inv_cond.append(1.0 / (2.0 + sig[j] / (t - 0.5)))
        mass.append(h27 + h47 * (sig[j] / (t * t + 0.1)))
    cond = [g_snow, g_snow, 1.0 / (half_snow + h14 * inv_cond[0])]
    for j in range(NLAY - NSNOW - 1):
        cond.append(1.0 / (h14 * (inv_cond[j] + inv_cond[j + 1])))
    g_bot = 1.0 / (h14 * inv_cond[-1])
    ratios = []
    values = []
    u = mass[0] + g_top
    held = mass[0] * temps[0]
    y = held + g_top * air + source_top
    for l in range(NLAY):
        below = cond[l] if l < NLAY - 1 else g_bot
        pivot = 1.0 / (u + below)
        ratio = below * pivot
        if l < NLAY - 1:
            ratios.append(ratio)
            values.append(y * pivot)
            u = mass[l + 1] + ratio * u
            mt = mass[l + 1] * temps[l + 1]
            held = held + mt
            y = mt + ratio * y
        else:
            last = y * pivot + ratio * ocean
    solved = [last]
    for l in range(NLAY - 2, -1, -1):
        solved.insert(0, values[l] + ratios[l] * solved[0])
    bottom = share * (g_bot * (last - ocean))
    top = share * (g_top * (air - solved[0]))
    light = share * jnp.exp2((-5.0 * LOG2E) * snow_depth - (1.5 * LOG2E) * floe)
    return solved, (
        bottom,
        top,
        light,
        share * solved[0],
        share * snow_depth,
        share * floe,
        share * held,
        share,
    )


def column_kernel(warm, share, floe, drift, recv, new_warm, flux):
    first = pl.program_id(0) * 8
    half = pl.program_id(1)

    def tile(k, carry):
        lanes = pl.ds(pl.multiple_of(k * 128, 128), 128)
        kk = half * 4 + k

        def field(f):
            return recv[pl.ds(first * ROWS_OUT + f * 8 + kk, 8, stride=ROWS_OUT), :]

        ocean, salinity, air, source_top, snowfall, top_resist = [field(f) for f in range(NSEND)]
        filled = salinity > 0.25
        sig = [salinity * (0.02 + 0.01 * j) for j in range(NLAY - NSNOW)]
        snow_add = 0.3 * snowfall
        sums = None
        for c in range(NCAT):
            temps = [warm[c, l, :, lanes] for l in range(NLAY)]
            solved, terms = one_column(
                temps,
                share[c, :, lanes],
                floe[c, :, lanes],
                drift[c, :, lanes] + snow_add,
                (ocean, air, source_top, top_resist),
                sig,
            )
            for l in range(NLAY):
                new_warm[c, l, :, lanes] = jnp.where(filled, solved[l], temps[l])
            sums = terms if sums is None else tuple(a + b for a, b in zip(sums, terms))
        bottom, top, light, surface, snow, thick, held, total = sums
        back = (
            bottom,
            top,
            light,
            surface,
            snow,
            thick - 0.05 * bottom,
            0.05 * (held + top - bottom + source_top * total),
        )
        for f in range(NBACK):
            flux[pl.ds(f * 8 + kk, 8, stride=ROWS_BACK), :] = back[f]
        return carry

    lax.fori_loop(0, 4, tile, 0, unroll=True)


def columns(warm, share, floe, drift, recv):
    cls = pl.BlockSpec((NCAT, 8, 512), lambda g, h: (0, g, h))
    col = pl.BlockSpec((NCAT, NLAY, 8, 512), lambda g, h: (0, 0, g, h))
    return pl.pallas_call(
        column_kernel,
        grid=(4, 2),
        out_shape=(
            jax.ShapeDtypeStruct((NCAT, NLAY, 32, 1024), F32),
            jax.ShapeDtypeStruct((B * CAP * ROWS_BACK, 128), F32),
        ),
        in_specs=[col, cls, cls, cls, VSPEC],
        out_specs=(col, pl.BlockSpec((8 * ROWS_BACK, 128), lambda g, h: (g, 0))),
        name="columns",
    )(warm, share, floe, drift, vmem(recv))


def unpack_kernel(own, land, back, kept, out, tile, count, sems):
    start_count(count)
    slots = block_slots(own, land, count, range(B))
    group = lane_groups()
    copies = []
    for bx in range(4):
        rows = []
        for f in range(NBACK):
            blocks = []
            for b in range(4 * bx, 4 * bx + 4):
                v = back[pl.ds(pl.multiple_of(slots[b] * ROWS_BACK + f * 8, 8), 8), :]
                blocks.append(jnp.where(land[b] == 0, v, 0.0))
            rows.append(swap_groups(blocks, group))
        for q in range(4):
            at = pl.ds(32 * bx + q, 8, stride=4)
            for f in range(NBACK):
                v = rows[f][q]
                tile[f, at, :] = kept[0, at, :] * v if f == 2 else v
            tile[7, at, :] = kept[1, at, :] * rows[0][q]
        part = pl.ds(32 * bx, 32)
        copies.append(pltpu.make_async_copy(tile.at[:, part, :], out.at[:, part, :], sems.at[bx]))
        copies[-1].start()
    for copy in copies:
        copy.wait()


def unpack(own, land, back, kept):
    return pl.pallas_call(
        unpack_kernel,
        out_shape=jax.ShapeDtypeStruct((8, 128, 128), F32),
        in_specs=[SSPEC, SSPEC, VSPEC, VSPEC],
        out_specs=pl.BlockSpec(memory_space=pl.ANY),
        scratch_shapes=[
            pltpu.VMEM((8, 128, 128), F32),
            pltpu.SMEM((B,), jnp.int32),
            pltpu.SemaphoreType.DMA((4,)),
        ],
        name="unpack",
    )(own, land, *vmem(back, kept))


def prepare_kernel(land, vel, stress, drive, weight, pressure, fields, left, right):
    group = lax.broadcasted_iota(jnp.int32, (32, 128), 1) // 32
    fields[0:2] = vel[...]
    fields[2:5] = stress[...]
    for bx in range(4):
        at = pl.ds(32 * bx, 32)
        water = jnp.zeros((32, 128), F32)
        for by in range(4):
            water = jnp.where(group == by, (1 - land[4 * bx + by]).astype(F32), water)
        w = weight[at, :]
        scale = water / (w + 0.5)
        beta = 0.5 * scale
        fields[5, at, :] = pressure[at, :] * (1.0 / 3.0)
        fields[6, at, :] = scale * w
        fields[7, at, :] = 0.25 * beta
        fields[8, at, :] = beta * (drive[0, at, :] + drive[2, at, :])
        fields[9, at, :] = beta * (drive[1, at, :] + drive[3, at, :])
    piece = lax.broadcasted_iota(jnp.int32, (8, 128), 1) // 8
    for f in range(NF):
        to_left = jnp.zeros((8, 128), F32)
        to_right = jnp.zeros((8, 128), F32)
        for t in range(16):
            x = fields[f, 8 * t : 8 * t + 8, :]
            to_left = jnp.where(piece == t, turn(x, 8 * t), to_left)
            to_right = jnp.where(piece == t, turn(x, 8 * t + 8), to_right)
        left[f] = to_left
        right[f] = to_right


def turn(x, shift):
    shift = shift % 128
    return pltpu.roll(x, shift, 1) if shift else x


def prepare(land, vel, stress, drive, weight, pressure):
    edge = pltpu.VMEM((NF, 8, 128), F32)
    return pl.pallas_call(
        prepare_kernel,
        out_shape=(pltpu.VMEM((NF, 128, 128), F32), edge, edge),
        in_specs=[SSPEC] + [VSPEC] * 5,
        out_specs=(VSPEC, VSPEC, VSPEC),
        name="prepare",
    )(land, vel, stress, drive, weight, pressure)


def rows_kernel(fields, left, right, up, down):
    piece = lax.broadcasted_iota(jnp.int32, (8, 128), 1) // 8
    for dst, first, t in ((up, 0, 0), (down, 120, 15)):
        dst[0:NF] = fields[:, first : first + 8, :]
        for i, side in enumerate((left, right)):
            corner = jnp.zeros((8, 128), F32)
            for f in range(NF):
                corner = jnp.where(piece == f, turn(side[f], 8 * (f - t)), corner)
            dst[NF + i] = corner


def edge_rows(fields, left, right):
    edge = pltpu.VMEM((NF + 2, 8, 128), F32)
    return pl.pallas_call(
        rows_kernel,
        out_shape=(edge, edge),
        in_specs=[VSPEC] * 3,
        out_specs=(VSPEC, VSPEC),
        name="rows",
    )(*vmem(fields, left, right))


GUARD = 8


def evp_kernel(fields, left, right, top, bottom, vel_out, stress_out, ext):
    lane = lax.broadcasted_iota(jnp.int32, (8, 128), 1)
    zero = jnp.zeros((8, 128), F32)

    def beside(from_right, from_left):
        return jnp.where(lane < 8, from_right, jnp.where(lane >= 120, from_left, 0.0))

    for f in range(NF):
        for h in range(2):
            ext[f, h, 0:8, :] = zero
            ext[f, h, 152:160, :] = zero
        for edge, r in ((top, 8), (bottom, 144)):
            ext[f, 0, r : r + 8, :] = edge[f]
            ext[f, 1, r : r + 8, :] = beside(
                turn(edge[NF + 1], -8 * f), turn(edge[NF], 120 - 8 * f)
            )
        ext[f, 0, 16:144, :] = fields[f]
        for t in range(16):
            r = 16 + 8 * t
            ext[f, 1, r : r + 8, :] = beside(
                turn(right[f], -8 * t), turn(left[f], 120 - 8 * t)
            )

    def across(x):
        n0, n1 = turn(x[0], 127), turn(x[1], 127)
        p0, p1 = turn(x[0], 1), turn(x[1], 1)
        last = lane == 127
        first = lane == 0
        return (
            jnp.where(last, n1, n0) - jnp.where(first, p1, p0),
            jnp.where(last, n0, n1) - jnp.where(first, p0, p1),
        )

    def subcycle(step, carry):
        for t in range(18):
            r = GUARD + 8 * t
            here, down, up = pl.ds(r, 8), pl.ds(r + 1, 8), pl.ds(r - 1, 8)
            b = across([ext[1, h, here, :] for h in range(2)])
            c = across([ext[0, h, here, :] for h in range(2)])
            for h in range(2):
                a = ext[0, h, down, :] - ext[0, h, up, :]
                d = ext[1, h, down, :] - ext[1, h, up, :]
                plus = a + b[h]
                minus = a - b[h]
                shear = c[h] + d
                square = 0.25 * (plus * plus) + 0.0625 * (minus * minus + shear * shear) + 0.04
                p3 = ext[5, h, here, :]
                k = p3 * lax.rsqrt(square)
                ext[2, h, here, :] = (2.0 / 3.0) * ext[2, h, here, :] + (0.5 * k) * plus - p3
                ext[3, h, here, :] = (2.0 / 3.0) * ext[3, h, here, :] + (0.125 * k) * minus
                ext[4, h, here, :] = (2.0 / 3.0) * ext[4, h, here, :] + (0.0625 * k) * shear
        for t in range(18):
            r = GUARD + 8 * t
            here, down, up = pl.ds(r, 8), pl.ds(r + 1, 8), pl.ds(r - 1, 8)
            shear = across([ext[4, h, here, :] for h in range(2)])
            differ = across([ext[2, h, here, :] - ext[3, h, here, :] for h in range(2)])
            for h in range(2):
                force_x = (ext[2, h, down, :] + ext[3, h, down, :]) - (
                    ext[2, h, up, :] + ext[3, h, up, :]
                )
                force_x = force_x + 2.0 * shear[h]
                force_y = differ[h] + 2.0 * (ext[4, h, down, :] - ext[4, h, up, :])
                alpha = ext[6, h, here, :]
                beta = ext[7, h, here, :]
                east = ext[0, h, here, :]
                north = ext[1, h, here, :]
                ext[0, h, here, :] = (
                    alpha * (east + 0.15 * north) + beta * force_x + ext[8, h, here, :]
                )
                ext[1, h, here, :] = (
                    alpha * (north - 0.15 * east) + beta * force_y + ext[9, h, here, :]
                )
        return carry

    lax.fori_loop(0, SUB, subcycle, 0)
    for f in range(2):
        vel_out[f] = ext[f, 0, 16:144, :]
    for f in range(3):
        stress_out[f] = ext[2 + f, 0, 16:144, :]


def evp(fields, left, right, top, bottom):
    return pl.pallas_call(
        evp_kernel,
        out_shape=(
            jax.ShapeDtypeStruct((2, 128, 128), F32),
            jax.ShapeDtypeStruct((3, 128, 128), F32),
        ),
        in_specs=[VSPEC] * 5,
        out_specs=(VSPEC, VSPEC),
        scratch_shapes=[pltpu.VMEM((NF, 2, 160, 128), F32)],
        name="evp",
    )(*vmem(fields, left, right, top, bottom))


def exchange(axis, to_lower, to_upper):
    peers = lax.axis_size(axis)
    up = [(i, i + 1) for i in range(peers - 1)]
    down = [(i + 1, i) for i in range(peers - 1)]
    from_lower = lax.ppermute(to_upper, axis, up)
    from_upper = lax.ppermute(to_lower, axis, down)
    return from_lower, from_upper


def swap(payload, rows):
    n = lax.axis_size("gy")
    out = lax.all_to_all(
        payload.reshape(n, CAP * rows, 128), "gy", split_axis=0, concat_axis=0, tiled=True
    )
    return out.reshape(n * CAP * rows, 128)


def step(
    conditions,
    warmth,
    share,
    floe,
    drift,
    velocity,
    stress,
    drive,
    weight,
    pressure,
    holder,
    land,
):
    own = holder.reshape(B)
    payload, kept = pack(own, land, conditions)
    recv = swap(payload, ROWS_OUT)

    fields, to_left, to_right = prepare(land, velocity, stress, drive, weight, pressure)
    left, right = exchange("gy", to_left, to_right)

    new_warm, flux = columns(
        warmth.transpose(1, 2, 0, 3),
        share.transpose(1, 0, 2),
        floe.transpose(1, 0, 2),
        drift.transpose(1, 0, 2),
        recv,
    )
    back = swap(flux, ROWS_BACK)
    first_rows, last_rows = edge_rows(fields, left, right)
    top, bottom = exchange("gx", first_rows, last_rows)
    velocity_new, stress_new = evp(fields, left, right, top, bottom)
    exchanges = unpack(own, land, back, kept)
    return (new_warm.transpose(2, 0, 1, 3), exchanges, velocity_new, stress_new)


def solution(mesh):
    return jax.shard_map(
        step,
        mesh=mesh,
        in_specs=(
            P(None, "gx", "gy"),
            P(("gx", "gy"), None, None, None),
            P(("gx", "gy"), None, None),
            P(("gx", "gy"), None, None),
            P(("gx", "gy"), None, None),
            P(None, "gx", "gy"),
            P(None, "gx", "gy"),
            P(None, "gx", "gy"),
            P("gx", "gy"),
            P("gx", "gy"),
            P(("gx", "gy"), None),
            P(("gx", "gy")),
        ),
        out_specs=(
            P(("gx", "gy"), None, None, None),
            P(None, "gx", "gy"),
            P(None, "gx", "gy"),
            P(None, "gx", "gy"),
        ),
        check_vma=False,
    )
```

```python
import jax
import jax.numpy as jnp
from jax import lax
from jax.experimental import pallas as pl
from jax.experimental.pallas import tpu as pltpu
from jax.sharding import PartitionSpec as P


B = 16
CAP = 2
NSEND = 6
NBACK = 7
NF = 10
SUB = 4
NCAT = 5
NLAY = 10
NSNOW = 3
ROWS_OUT = NSEND * 8
ROWS_BACK = NBACK * 8

F32 = jnp.float32
LOG2E = 1.4426950408889634
VSPEC = pl.BlockSpec(memory_space=pltpu.VMEM)
SSPEC = pl.BlockSpec(memory_space=pltpu.SMEM)


def vmem(*arrays):
    out = [pltpu.with_memory_space_constraint(a, pltpu.VMEM) for a in arrays]
    return out if len(out) > 1 else out[0]


def lane_groups():
    return lax.broadcasted_iota(jnp.int32, (8, 128), 1) // 32


def swap_groups(rows, group):
    low = group < 2
    even = (group & 1) == 0
    v0, v1, v2, v3 = rows

    def roll(x, s):
        return pltpu.roll(x, s, 1)

    a0 = jnp.where(low, v0, roll(v2, 64))
    a2 = jnp.where(low, roll(v0, 64), v2)
    a1 = jnp.where(low, v1, roll(v3, 64))
    a3 = jnp.where(low, roll(v1, 64), v3)
    return (
        jnp.where(even, a0, roll(a1, 32)),
        jnp.where(even, roll(a0, 96), a1),
        jnp.where(even, a2, roll(a3, 32)),
        jnp.where(even, roll(a2, 96), a3),
    )


def block_slots(own, land, count, blocks):
    slots = []
    for b in blocks:
        o = own[b]
        r = count[o]
        slots.append(jnp.minimum(o * CAP + r, B * CAP - 1))
        count[o] = r + 1 - land[b]
    return slots


def start_count(count):
    for o in range(B):
        count[o] = 0


def pack_kernel(own, land, x, out, kept, count):
    out[...] = jnp.zeros_like(out)
    kept[0] = 0.7 * x[3]
    kept[1] = -0.05 * x[1]
    start_count(count)
    slots = block_slots(own, land, count, range(B))
    group = lane_groups()
    for bx in range(4):

        def rows(f):
            return [x[f, pl.ds(32 * bx + q, 8, stride=4), :] for q in range(4)]

        visible, near_red, longwave = rows(3), rows(4), rows(5)
        fields = [
            rows(0),
            rows(1),
            rows(2),
            [0.25 * a + 0.45 * b + 0.3 * c for a, b, c in zip(visible, near_red, longwave)],
            rows(6),
            [1.0 / (1.0 + 2.0 * w) for w in rows(7)],
        ]
        blocks = [swap_groups(r, group) for r in fields]
        for by in range(4):
            b = 4 * bx + by

            @pl.when(land[b] == 0)
            def _():
                for f in range(NSEND):
                    out[pl.ds(pl.multiple_of(slots[b] * ROWS_OUT + f * 8, 8), 8), :] = blocks[f][by]


def pack(own, land, conditions):
    return pl.pallas_call(
        pack_kernel,
        out_shape=(pltpu.VMEM((B * CAP * ROWS_OUT, 128), F32), pltpu.VMEM((2, 128, 128), F32)),
        in_specs=[SSPEC, SSPEC, VSPEC],
        out_specs=(VSPEC, VSPEC),
        scratch_shapes=[pltpu.SMEM((B,), jnp.int32)],
        name="pack",
    )(own, land, conditions)


def one_column(temps, share, floe, snow_depth, forcing, sig):
    ocean, air, source_top, top_resist = forcing
    h14 = floe * (1.0 / 14.0)
    h27 = floe * (2.0 / 7.0)
    h47 = floe * (4.0 / 7.0)
    m_snow = snow_depth * (2.0 / 3.0)
    half_snow = snow_depth * (0.5 / 0.9)
    g_snow = 0.9 / snow_depth
    g_top = 1.0 / (half_snow + top_resist)
    inv_cond = []
    mass = [m_snow] * NSNOW
    for j in range(NLAY - NSNOW):
        t = temps[NSNOW + j]
        inv_cond.append(1.0 / (2.0 + sig[j] / (t - 0.5)))
        mass.append(h27 + h47 * (sig[j] / (t * t + 0.1)))
    cond = [g_snow, g_snow, 1.0 / (half_snow + h14 * inv_cond[0])]
    for j in range(NLAY - NSNOW - 1):
        cond.append(1.0 / (h14 * (inv_cond[j] + inv_cond[j + 1])))
    g_bot = 1.0 / (h14 * inv_cond[-1])
    ratios = []
    values = []
    u = mass[0] + g_top
    held = mass[0] * temps[0]
    y = held + g_top * air + source_top
    for l in range(NLAY):
        below = cond[l] if l < NLAY - 1 else g_bot
        pivot = 1.0 / (u + below)
        ratio = below * pivot
        if l < NLAY - 1:
            ratios.append(ratio)
            values.append(y * pivot)
            u = mass[l + 1] + ratio * u
            mt = mass[l + 1] * temps[l + 1]
            held = held + mt
            y = mt + ratio * y
        else:
            last = y * pivot + ratio * ocean
    solved = [last]
    for l in range(NLAY - 2, -1, -1):
        solved.insert(0, values[l] + ratios[l] * solved[0])
    bottom = share * (g_bot * (last - ocean))
    top = share * (g_top * (air - solved[0]))
    light = share * jnp.exp2((-5.0 * LOG2E) * snow_depth - (1.5 * LOG2E) * floe)
    return solved, (
        bottom,
        top,
        light,
        share * solved[0],
        share * snow_depth,
        share * floe,
        share * held,
        share,
    )


HBM = pl.BlockSpec(memory_space=pltpu.HBM)
CHUNKS = 8
CHUNK = 512


def chunk_at(s):
    rows = pl.ds(pl.multiple_of(s // 2 * 8, 8), 8)
    lanes = pl.ds(pl.multiple_of(s % 2 * CHUNK, CHUNK), CHUNK)
    return rows, lanes


def fetches(s, warm, classes, warm_to, classes_to, sems):
    rows, lanes = chunk_at(s)
    return [pltpu.make_async_copy(warm.at[:, :, rows, lanes], warm_to, sems.at[3])] + [
        pltpu.make_async_copy(src.at[:, rows, lanes], classes_to.at[i], sems.at[i])
        for i, src in enumerate(classes)
    ]


def column_kernel(
    warm, share, floe, drift, warm0, classes0, recv, new_warm, flux, wbuf, cbuf, obuf, fbuf, insem, outsem, fsem
):
    classes = (share, floe, drift)

    def fetch(s, slot):
        return fetches(s, warm, classes, wbuf.at[slot], cbuf.at[slot], insem.at[slot])

    def put(s, slot):
        rows, lanes = chunk_at(s)
        return pltpu.make_async_copy(obuf.at[slot], new_warm.at[:, :, rows, lanes], outsem.at[slot])

    def put_flux(g):
        part = pl.ds(pl.multiple_of(g * 8 * ROWS_BACK, 8), 8 * ROWS_BACK)
        return pltpu.make_async_copy(fbuf.at[part, :], flux.at[part, :], fsem.at[g])

    def compute(s, warm_in, classes_in, out):
        first = s // 2 * 8

        def tile(k, carry):
            kk = s % 2 * 4 + k
            lanes = pl.ds(pl.multiple_of(k * 128, 128), 128)

            def field(f):
                return recv[pl.ds(first * ROWS_OUT + f * 8 + kk, 8, stride=ROWS_OUT), :]

            ocean, salinity, air, source_top, snowfall, top_resist = [
                field(f) for f in range(NSEND)
            ]
            filled = salinity > 0.25
            sig = [salinity * (0.02 + 0.01 * j) for j in range(NLAY - NSNOW)]
            snow_add = 0.3 * snowfall
            sums = None
            for c in range(NCAT):
                temps = [warm_in[c, l, :, lanes] for l in range(NLAY)]
                solved, terms = one_column(
                    temps,
                    classes_in[0, c, :, lanes],
                    classes_in[1, c, :, lanes],
                    classes_in[2, c, :, lanes] + snow_add,
                    (ocean, air, source_top, top_resist),
                    sig,
                )
                for l in range(NLAY):
                    out[c, l, :, lanes] = jnp.where(filled, solved[l], temps[l])
                sums = terms if sums is None else tuple(a + b for a, b in zip(sums, terms))
            bottom, top, light, surface, snow, thick, held, total = sums
            back = (
                bottom,
                top,
                light,
                surface,
                snow,
                thick - 0.05 * bottom,
                0.05 * (held + top - bottom + source_top * total),
            )
            for f in range(NBACK):
                fbuf[pl.ds(first * ROWS_BACK + f * 8 + kk, 8, stride=ROWS_BACK), :] = back[f]
            return carry

        lax.fori_loop(0, 4, tile, 0, unroll=True)

    def start(copies):
        for copy in copies:
            copy.start()

    def wait(copies):
        for copy in copies:
            copy.wait()

    start(fetch(1, 1))
    start(fetch(2, 0))
    compute(0, warm0, classes0, obuf.at[0])
    put(0, 0).start()

    def chunk(s, carry):
        slot = s % 2
        wait(fetch(s, slot))

        @pl.when(s >= 2)
        def _():
            put(s - 2, slot).wait()

        compute(s, wbuf.at[slot], cbuf.at[slot], obuf.at[slot])
        put(s, slot).start()

        @pl.when(slot == 1)
        def _():
            put_flux(s // 2).start()

        @pl.when(s + 2 < CHUNKS)
        def _():
            start(fetch(s + 2, slot))

        return carry

    lax.fori_loop(1, CHUNKS, chunk, 0)
    put(CHUNKS - 2, 0).wait()
    put(CHUNKS - 1, 1).wait()
    for g in range(CHUNKS // 2):
        put_flux(g).wait()


def columns(warm, share, floe, drift, warm0, classes0, recv):
    return pl.pallas_call(
        column_kernel,
        out_shape=(
            jax.ShapeDtypeStruct((NCAT, NLAY, 32, 1024), F32),
            jax.ShapeDtypeStruct((B * CAP * ROWS_BACK, 128), F32),
        ),
        in_specs=[HBM] * 4 + [VSPEC] * 3,
        out_specs=(HBM, HBM),
        scratch_shapes=[
            pltpu.VMEM((2, NCAT, NLAY, 8, CHUNK), F32),
            pltpu.VMEM((2, 3, NCAT, 8, CHUNK), F32),
            pltpu.VMEM((2, NCAT, NLAY, 8, CHUNK), F32),
            pltpu.VMEM((B * CAP * ROWS_BACK, 128), F32),
            pltpu.SemaphoreType.DMA((2, 4)),
            pltpu.SemaphoreType.DMA((2,)),
            pltpu.SemaphoreType.DMA((4,)),
        ],
        name="columns",
    )(warm, share, floe, drift, *vmem(warm0, classes0, recv))


def unpack_kernel(own, land, back, kept, out, tile, count, sems):
    start_count(count)
    slots = block_slots(own, land, count, range(B))
    group = lane_groups()
    copies = []
    for bx in range(4):
        rows = []
        for f in range(NBACK):
            blocks = []
            for b in range(4 * bx, 4 * bx + 4):
                v = back[pl.ds(pl.multiple_of(slots[b] * ROWS_BACK + f * 8, 8), 8), :]
                blocks.append(jnp.where(land[b] == 0, v, 0.0))
            rows.append(swap_groups(blocks, group))
        for q in range(4):
            at = pl.ds(32 * bx + q, 8, stride=4)
            for f in range(NBACK):
                v = rows[f][q]
                tile[f, at, :] = kept[0, at, :] * v if f == 2 else v
            tile[7, at, :] = kept[1, at, :] * rows[0][q]
        part = pl.ds(32 * bx, 32)
        copies.append(pltpu.make_async_copy(tile.at[:, part, :], out.at[:, part, :], sems.at[bx]))
        copies[-1].start()
    for copy in copies:
        copy.wait()


def unpack(own, land, back, kept):
    return pl.pallas_call(
        unpack_kernel,
        out_shape=jax.ShapeDtypeStruct((8, 128, 128), F32),
        in_specs=[SSPEC, SSPEC, VSPEC, VSPEC],
        out_specs=pl.BlockSpec(memory_space=pl.ANY),
        scratch_shapes=[
            pltpu.VMEM((8, 128, 128), F32),
            pltpu.SMEM((B,), jnp.int32),
            pltpu.SemaphoreType.DMA((4,)),
        ],
        name="unpack",
    )(own, land, *vmem(back, kept))


def prepare_kernel(
    land, vel, stress, drive, weight, pressure, warm, share, floe, drift,
    fields, left, right, up, down, warm0, classes0, sems,
):
    copies = fetches(0, warm, (share, floe, drift), warm0, classes0, sems)
    for copy in copies:
        copy.start()
    group = lax.broadcasted_iota(jnp.int32, (32, 128), 1) // 32
    fields[0:2] = vel[...]
    fields[2:5] = stress[...]
    for bx in range(4):
        at = pl.ds(32 * bx, 32)
        water = jnp.zeros((32, 128), F32)
        for by in range(4):
            water = jnp.where(group == by, (1 - land[4 * bx + by]).astype(F32), water)
        w = weight[at, :]
        scale = water / (w + 0.5)
        beta = 0.5 * scale
        fields[5, at, :] = pressure[at, :] * (1.0 / 3.0)
        fields[6, at, :] = scale * w
        fields[7, at, :] = 0.25 * beta
        fields[8, at, :] = beta * (drive[0, at, :] + drive[2, at, :])
        fields[9, at, :] = beta * (drive[1, at, :] + drive[3, at, :])
    piece = lax.broadcasted_iota(jnp.int32, (8, 128), 1) // 8
    for f in range(NF):
        to_left = jnp.zeros((8, 128), F32)
        to_right = jnp.zeros((8, 128), F32)
        for t in range(16):
            x = fields[f, 8 * t : 8 * t + 8, :]
            to_left = jnp.where(piece == t, turn(x, 8 * t), to_left)
            to_right = jnp.where(piece == t, turn(x, 8 * t + 8), to_right)
        left[f] = to_left
        right[f] = to_right
    up[...] = fields[:, 0:8, :]
    down[...] = fields[:, 120:128, :]
    for copy in copies:
        copy.wait()


def turn(x, shift):
    shift = shift % 128
    return pltpu.roll(x, shift, 1) if shift else x


def prepare(land, vel, stress, drive, weight, pressure, *columns_in):
    edge = pltpu.VMEM((NF, 8, 128), F32)
    return pl.pallas_call(
        prepare_kernel,
        out_shape=(
            jax.ShapeDtypeStruct((NF, 128, 128), F32),
            edge,
            edge,
            edge,
            edge,
            pltpu.VMEM((NCAT, NLAY, 8, CHUNK), F32),
            pltpu.VMEM((3, NCAT, 8, CHUNK), F32),
        ),
        in_specs=[SSPEC] + [VSPEC] * 5 + [HBM] * 4,
        out_specs=(VSPEC,) * 7,
        scratch_shapes=[pltpu.SemaphoreType.DMA((4,))],
        name="prepare",
    )(land, vel, stress, drive, weight, pressure, *columns_in)


def rows_kernel(first_rows, last_rows, left, right, up, down):
    piece = lax.broadcasted_iota(jnp.int32, (8, 128), 1) // 8
    for dst, src, t in ((up, first_rows, 0), (down, last_rows, 15)):
        dst[0:NF] = src[...]
        for i, side in enumerate((left, right)):
            corner = jnp.zeros((8, 128), F32)
            for f in range(NF):
                corner = jnp.where(piece == f, turn(side[f], 8 * (f - t)), corner)
            dst[NF + i] = corner


def edge_rows(first_rows, last_rows, left, right):
    edge = pltpu.VMEM((NF + 2, 8, 128), F32)
    return pl.pallas_call(
        rows_kernel,
        out_shape=(edge, edge),
        in_specs=[VSPEC] * 4,
        out_specs=(VSPEC, VSPEC),
        name="rows",
    )(*vmem(first_rows, last_rows, left, right))


def stage_kernel(fields, _, staged, sem):
    copy = pltpu.make_async_copy(fields, staged, sem)
    copy.start()
    copy.wait()


def stage(fields, after):
    return pl.pallas_call(
        stage_kernel,
        out_shape=pltpu.VMEM((NF, 128, 128), F32),
        in_specs=[HBM, VSPEC],
        out_specs=VSPEC,
        scratch_shapes=[pltpu.SemaphoreType.DMA(())],
        name="stage",
    )(fields, vmem(after))


GUARD = 8


def evp_kernel(fields, left, right, top, bottom, vel_out, stress_out, ext):
    lane = lax.broadcasted_iota(jnp.int32, (8, 128), 1)
    zero = jnp.zeros((8, 128), F32)

    def beside(from_right, from_left):
        return jnp.where(lane < 8, from_right, jnp.where(lane >= 120, from_left, 0.0))

    for f in range(NF):
        for h in range(2):
            ext[f, h, 0:8, :] = zero
            ext[f, h, 152:160, :] = zero
        for edge, r in ((top, 8), (bottom, 144)):
            ext[f, 0, r : r + 8, :] = edge[f]
            ext[f, 1, r : r + 8, :] = beside(
                turn(edge[NF + 1], -8 * f), turn(edge[NF], 120 - 8 * f)
            )
        ext[f, 0, 16:144, :] = fields[f]
        for t in range(16):
            r = 16 + 8 * t
            ext[f, 1, r : r + 8, :] = beside(
                turn(right[f], -8 * t), turn(left[f], 120 - 8 * t)
            )

    def across(x):
        n0, n1 = turn(x[0], 127), turn(x[1], 127)
        p0, p1 = turn(x[0], 1), turn(x[1], 1)
        last = lane == 127
        first = lane == 0
        return (
            jnp.where(last, n1, n0) - jnp.where(first, p1, p0),
            jnp.where(last, n0, n1) - jnp.where(first, p0, p1),
        )

    def subcycle(step, carry):
        for t in range(18):
            r = GUARD + 8 * t
            here, down, up = pl.ds(r, 8), pl.ds(r + 1, 8), pl.ds(r - 1, 8)
            b = across([ext[1, h, here, :] for h in range(2)])
            c = across([ext[0, h, here, :] for h in range(2)])
            for h in range(2):
                a = ext[0, h, down, :] - ext[0, h, up, :]
                d = ext[1, h, down, :] - ext[1, h, up, :]
                plus = a + b[h]
                minus = a - b[h]
                shear = c[h] + d
                square = 0.25 * (plus * plus) + 0.0625 * (minus * minus + shear * shear) + 0.04
                p3 = ext[5, h, here, :]
                k = p3 * lax.rsqrt(square)
                ext[2, h, here, :] = (2.0 / 3.0) * ext[2, h, here, :] + (0.5 * k) * plus - p3
                ext[3, h, here, :] = (2.0 / 3.0) * ext[3, h, here, :] + (0.125 * k) * minus
                ext[4, h, here, :] = (2.0 / 3.0) * ext[4, h, here, :] + (0.0625 * k) * shear
        for t in range(18):
            r = GUARD + 8 * t
            here, down, up = pl.ds(r, 8), pl.ds(r + 1, 8), pl.ds(r - 1, 8)
            shear = across([ext[4, h, here, :] for h in range(2)])
            differ = across([ext[2, h, here, :] - ext[3, h, here, :] for h in range(2)])
            for h in range(2):
                force_x = (ext[2, h, down, :] + ext[3, h, down, :]) - (
                    ext[2, h, up, :] + ext[3, h, up, :]
                )
                force_x = force_x + 2.0 * shear[h]
                force_y = differ[h] + 2.0 * (ext[4, h, down, :] - ext[4, h, up, :])
                alpha = ext[6, h, here, :]
                beta = ext[7, h, here, :]
                east = ext[0, h, here, :]
                north = ext[1, h, here, :]
                ext[0, h, here, :] = (
                    alpha * (east + 0.15 * north) + beta * force_x + ext[8, h, here, :]
                )
                ext[1, h, here, :] = (
                    alpha * (north - 0.15 * east) + beta * force_y + ext[9, h, here, :]
                )
        return carry

    lax.fori_loop(0, SUB, subcycle, 0)
    for f in range(2):
        vel_out[f] = ext[f, 0, 16:144, :]
    for f in range(3):
        stress_out[f] = ext[2 + f, 0, 16:144, :]


def evp(fields, left, right, top, bottom):
    return pl.pallas_call(
        evp_kernel,
        out_shape=(
            jax.ShapeDtypeStruct((2, 128, 128), F32),
            jax.ShapeDtypeStruct((3, 128, 128), F32),
        ),
        in_specs=[VSPEC] * 5,
        out_specs=(VSPEC, VSPEC),
        scratch_shapes=[pltpu.VMEM((NF, 2, 160, 128), F32)],
        name="evp",
    )(*vmem(fields, left, right, top, bottom))


def exchange(axis, to_lower, to_upper):
    peers = lax.axis_size(axis)
    up = [(i, i + 1) for i in range(peers - 1)]
    down = [(i + 1, i) for i in range(peers - 1)]
    from_lower = lax.ppermute(to_upper, axis, up)
    from_upper = lax.ppermute(to_lower, axis, down)
    return from_lower, from_upper


def swap(payload, rows):
    n = lax.axis_size("gy")
    out = lax.all_to_all(
        payload.reshape(n, CAP * rows, 128), "gy", split_axis=0, concat_axis=0, tiled=True
    )
    return out.reshape(n * CAP * rows, 128)


def step(
    conditions,
    warmth,
    share,
    floe,
    drift,
    velocity,
    stress,
    drive,
    weight,
    pressure,
    holder,
    land,
):
    own = holder.reshape(B)
    payload, kept = pack(own, land, conditions)
    recv = swap(payload, ROWS_OUT)

    columns_in = (
        warmth.transpose(1, 2, 0, 3),
        share.transpose(1, 0, 2),
        floe.transpose(1, 0, 2),
        drift.transpose(1, 0, 2),
    )
    fields, to_left, to_right, first, last, warm0, classes0 = prepare(
        land, velocity, stress, drive, weight, pressure, *columns_in
    )
    left, right = exchange("gy", to_left, to_right)

    new_warm, flux = columns(*columns_in, warm0, classes0, recv)
    back = swap(flux, ROWS_BACK)
    first_rows, last_rows = edge_rows(first, last, left, right)
    top, bottom = exchange("gx", first_rows, last_rows)
    fields = stage(fields, first_rows)
    velocity_new, stress_new = evp(fields, left, right, top, bottom)
    exchanges = unpack(own, land, back, kept)
    return (new_warm.transpose(2, 0, 1, 3), exchanges, velocity_new, stress_new)


def solution(mesh):
    return jax.shard_map(
        step,
        mesh=mesh,
        in_specs=(
            P(None, "gx", "gy"),
            P(("gx", "gy"), None, None, None),
            P(("gx", "gy"), None, None),
            P(("gx", "gy"), None, None),
            P(("gx", "gy"), None, None),
            P(None, "gx", "gy"),
            P(None, "gx", "gy"),
            P(None, "gx", "gy"),
            P("gx", "gy"),
            P("gx", "gy"),
            P(("gx", "gy"), None),
            P(("gx", "gy")),
        ),
        out_specs=(
            P(("gx", "gy"), None, None, None),
            P(None, "gx", "gy"),
            P(None, "gx", "gy"),
            P(None, "gx", "gy"),
        ),
        check_vma=False,
    )
```

```python
import jax
import jax.numpy as jnp
from jax import lax
from jax.experimental import pallas as pl
from jax.experimental.pallas import tpu as pltpu
from jax.sharding import PartitionSpec as P


B = 16
CAP = 2
NSEND = 6
NBACK = 7
NF = 10
SUB = 4
NCAT = 5
NLAY = 10
NSNOW = 3
ROWS_OUT = NSEND * 8
ROWS_BACK = NBACK * 8

F32 = jnp.float32
LOG2E = 1.4426950408889634
VSPEC = pl.BlockSpec(memory_space=pltpu.VMEM)
SSPEC = pl.BlockSpec(memory_space=pltpu.SMEM)
HBM = pl.BlockSpec(memory_space=pltpu.HBM)


def vmem(*arrays):
    out = [pltpu.with_memory_space_constraint(a, pltpu.VMEM) for a in arrays]
    return out if len(out) > 1 else out[0]


def lane_groups():
    return lax.broadcasted_iota(jnp.int32, (8, 128), 1) // 32


def swap_groups(rows, group):
    low = group < 2
    even = (group & 1) == 0
    v0, v1, v2, v3 = rows

    def roll(x, s):
        return pltpu.roll(x, s, 1)

    a0 = jnp.where(low, v0, roll(v2, 64))
    a2 = jnp.where(low, roll(v0, 64), v2)
    a1 = jnp.where(low, v1, roll(v3, 64))
    a3 = jnp.where(low, roll(v1, 64), v3)
    return (
        jnp.where(even, a0, roll(a1, 32)),
        jnp.where(even, roll(a0, 96), a1),
        jnp.where(even, a2, roll(a3, 32)),
        jnp.where(even, roll(a2, 96), a3),
    )


def block_slots(own, land, count, blocks):
    slots = []
    for b in blocks:
        o = own[b]
        r = count[o]
        slots.append(jnp.minimum(o * CAP + r, B * CAP - 1))
        count[o] = r + 1 - land[b]
    return slots


def start_count(count):
    for o in range(B):
        count[o] = 0


def pack_kernel(own, land, x_hbm, out, kept, x, staged, count, taken, insem, outsem):
    reads = []
    for bx in range(4):
        part = pl.ds(32 * bx, 32)
        reads.append(pltpu.make_async_copy(x_hbm.at[:, part, :], x.at[:, part, :], insem.at[bx]))
        reads[-1].start()
    zeros = pl.ds(B * ROWS_OUT, ROWS_OUT)
    staged[zeros, :] = jnp.zeros((ROWS_OUT, 128), F32)
    start_count(count)
    slots = block_slots(own, land, count, range(B))
    for s in range(B * CAP):
        taken[s] = 0
    for b in range(B):

        @pl.when(land[b] == 0)
        def _():
            taken[slots[b]] = 1

    def send(source, slot):
        rows = pl.ds(pl.multiple_of(slot * ROWS_OUT, 8), ROWS_OUT)
        pltpu.make_async_copy(staged.at[source, :], out.at[rows, :], outsem).start()

    for s in range(B * CAP):

        @pl.when(taken[s] == 0)
        def _():
            send(zeros, s)

    group = lane_groups()
    for bx in range(4):
        reads[bx].wait()

        def rows(f):
            return [x[f, pl.ds(32 * bx + q, 8, stride=4), :] for q in range(4)]

        visible, near_red, longwave = rows(3), rows(4), rows(5)
        fields = [
            rows(0),
            rows(1),
            rows(2),
            [0.25 * a + 0.45 * b + 0.3 * c for a, b, c in zip(visible, near_red, longwave)],
            rows(6),
            [1.0 / (1.0 + 2.0 * w) for w in rows(7)],
        ]
        blocks = [swap_groups(r, group) for r in fields]
        for by in range(4):
            b = 4 * bx + by
            for f in range(NSEND):
                staged[b * ROWS_OUT + f * 8 : b * ROWS_OUT + f * 8 + 8, :] = blocks[f][by]

            @pl.when(land[b] == 0)
            def _():
                send(pl.ds(b * ROWS_OUT, ROWS_OUT), slots[b])

    kept[0] = 0.7 * x[3]
    kept[1] = -0.05 * x[1]
    whole = pl.ds(0, B * CAP * ROWS_OUT)
    pltpu.make_async_copy(out.at[whole, :], out.at[whole, :], outsem).wait()


def pack(own, land, conditions):
    return pl.pallas_call(
        pack_kernel,
        out_shape=(
            jax.ShapeDtypeStruct((B * CAP * ROWS_OUT, 128), F32),
            pltpu.VMEM((2, 128, 128), F32),
        ),
        in_specs=[SSPEC, SSPEC, HBM],
        out_specs=(HBM, VSPEC),
        scratch_shapes=[
            pltpu.VMEM((8, 128, 128), F32),
            pltpu.VMEM(((B + 1) * ROWS_OUT, 128), F32),
            pltpu.SMEM((B,), jnp.int32),
            pltpu.SMEM((B * CAP,), jnp.int32),
            pltpu.SemaphoreType.DMA((4,)),
            pltpu.SemaphoreType.DMA(()),
        ],
        name="pack",
    )(own, land, conditions)


def one_column(temps, share, floe, snow_depth, forcing, sig):
    ocean, air, source_top, top_resist = forcing
    h14 = floe * (1.0 / 14.0)
    h27 = floe * (2.0 / 7.0)
    h47 = floe * (4.0 / 7.0)
    m_snow = snow_depth * (2.0 / 3.0)
    half_snow = snow_depth * (0.5 / 0.9)
    g_snow = 0.9 / snow_depth
    g_top = 1.0 / (half_snow + top_resist)
    inv_cond = []
    mass = [m_snow] * NSNOW
    for j in range(NLAY - NSNOW):
        t = temps[NSNOW + j]
        inv_cond.append(1.0 / (2.0 + sig[j] / (t - 0.5)))
        mass.append(h27 + h47 * (sig[j] / (t * t + 0.1)))
    cond = [g_snow, g_snow, 1.0 / (half_snow + h14 * inv_cond[0])]
    for j in range(NLAY - NSNOW - 1):
        cond.append(1.0 / (h14 * (inv_cond[j] + inv_cond[j + 1])))
    g_bot = 1.0 / (h14 * inv_cond[-1])
    ratios = []
    values = []
    u = mass[0] + g_top
    held = mass[0] * temps[0]
    y = held + g_top * air + source_top
    for l in range(NLAY):
        below = cond[l] if l < NLAY - 1 else g_bot
        pivot = 1.0 / (u + below)
        ratio = below * pivot
        if l < NLAY - 1:
            ratios.append(ratio)
            values.append(y * pivot)
            u = mass[l + 1] + ratio * u
            mt = mass[l + 1] * temps[l + 1]
            held = held + mt
            y = mt + ratio * y
        else:
            last = y * pivot + ratio * ocean
    solved = [last]
    for l in range(NLAY - 2, -1, -1):
        solved.insert(0, values[l] + ratios[l] * solved[0])
    bottom = share * (g_bot * (last - ocean))
    top = share * (g_top * (air - solved[0]))
    light = share * jnp.exp2((-5.0 * LOG2E) * snow_depth - (1.5 * LOG2E) * floe)
    return solved, (
        bottom,
        top,
        light,
        share * solved[0],
        share * snow_depth,
        share * floe,
        share * held,
        share,
    )


CHUNKS = 8
CHUNK = 512


def chunk_at(s):
    rows = pl.ds(pl.multiple_of(s // 2 * 8, 8), 8)
    lanes = pl.ds(pl.multiple_of(s % 2 * CHUNK, CHUNK), CHUNK)
    return rows, lanes


def fetches(s, warm, classes, warm_to, classes_to, sems):
    rows, lanes = chunk_at(s)
    return [pltpu.make_async_copy(warm.at[:, :, rows, lanes], warm_to, sems.at[3])] + [
        pltpu.make_async_copy(src.at[:, rows, lanes], classes_to.at[i], sems.at[i])
        for i, src in enumerate(classes)
    ]


def column_kernel(
    warm, share, floe, drift, warm0, classes0, recv, new_warm, flux, wbuf, cbuf, obuf, fbuf, insem, outsem, fsem
):
    classes = (share, floe, drift)

    def fetch(s, slot):
        return fetches(s, warm, classes, wbuf.at[slot], cbuf.at[slot], insem.at[slot])

    def put(s, slot):
        rows, lanes = chunk_at(s)
        return pltpu.make_async_copy(obuf.at[slot], new_warm.at[:, :, rows, lanes], outsem.at[slot])

    def put_flux(g):
        part = pl.ds(pl.multiple_of(g * 8 * ROWS_BACK, 8), 8 * ROWS_BACK)
        return pltpu.make_async_copy(fbuf.at[part, :], flux.at[part, :], fsem.at[g])

    def compute(s, warm_in, classes_in, out):
        first = s // 2 * 8

        def tile(k, carry):
            kk = s % 2 * 4 + k
            lanes = pl.ds(pl.multiple_of(k * 128, 128), 128)

            def field(f):
                return recv[pl.ds(first * ROWS_OUT + f * 8 + kk, 8, stride=ROWS_OUT), :]

            ocean, salinity, air, source_top, snowfall, top_resist = [
                field(f) for f in range(NSEND)
            ]
            filled = salinity > 0.25
            sig = [salinity * (0.02 + 0.01 * j) for j in range(NLAY - NSNOW)]
            snow_add = 0.3 * snowfall
            sums = None
            for c in range(NCAT):
                temps = [warm_in[c, l, :, lanes] for l in range(NLAY)]
                solved, terms = one_column(
                    temps,
                    classes_in[0, c, :, lanes],
                    classes_in[1, c, :, lanes],
                    classes_in[2, c, :, lanes] + snow_add,
                    (ocean, air, source_top, top_resist),
                    sig,
                )
                for l in range(NLAY):
                    out[c, l, :, lanes] = jnp.where(filled, solved[l], temps[l])
                sums = terms if sums is None else tuple(a + b for a, b in zip(sums, terms))
            bottom, top, light, surface, snow, thick, held, total = sums
            back = (
                bottom,
                top,
                light,
                surface,
                snow,
                thick - 0.05 * bottom,
                0.05 * (held + top - bottom + source_top * total),
            )
            for f in range(NBACK):
                fbuf[pl.ds(first * ROWS_BACK + f * 8 + kk, 8, stride=ROWS_BACK), :] = back[f]
            return carry

        lax.fori_loop(0, 4, tile, 0, unroll=True)

    def start(copies):
        for copy in copies:
            copy.start()

    def wait(copies):
        for copy in copies:
            copy.wait()

    start(fetch(1, 1))
    start(fetch(2, 0))
    compute(0, warm0, classes0, obuf.at[0])
    put(0, 0).start()

    def chunk(s, carry):
        slot = s % 2
        wait(fetch(s, slot))

        @pl.when(s >= 2)
        def _():
            put(s - 2, slot).wait()

        compute(s, wbuf.at[slot], cbuf.at[slot], obuf.at[slot])
        put(s, slot).start()

        @pl.when(slot == 1)
        def _():
            put_flux(s // 2).start()

        @pl.when(s + 2 < CHUNKS)
        def _():
            start(fetch(s + 2, slot))

        return carry

    lax.fori_loop(1, CHUNKS, chunk, 0)
    put(CHUNKS - 2, 0).wait()
    put(CHUNKS - 1, 1).wait()
    for g in range(CHUNKS // 2):
        put_flux(g).wait()


def columns(warm, share, floe, drift, warm0, classes0, recv):
    return pl.pallas_call(
        column_kernel,
        out_shape=(
            jax.ShapeDtypeStruct((NCAT, NLAY, 32, 1024), F32),
            jax.ShapeDtypeStruct((B * CAP * ROWS_BACK, 128), F32),
        ),
        in_specs=[HBM] * 4 + [VSPEC] * 3,
        out_specs=(HBM, HBM),
        scratch_shapes=[
            pltpu.VMEM((2, NCAT, NLAY, 8, CHUNK), F32),
            pltpu.VMEM((2, 3, NCAT, 8, CHUNK), F32),
            pltpu.VMEM((2, NCAT, NLAY, 8, CHUNK), F32),
            pltpu.VMEM((B * CAP * ROWS_BACK, 128), F32),
            pltpu.SemaphoreType.DMA((2, 4)),
            pltpu.SemaphoreType.DMA((2,)),
            pltpu.SemaphoreType.DMA((4,)),
        ],
        name="columns",
    )(warm, share, floe, drift, *vmem(warm0, classes0, recv))


def unpack_kernel(own, land, back, kept, out, tile, count, sems):
    start_count(count)
    slots = block_slots(own, land, count, range(B))
    group = lane_groups()
    copies = []
    for bx in range(4):
        rows = []
        for f in range(NBACK):
            blocks = []
            for b in range(4 * bx, 4 * bx + 4):
                v = back[pl.ds(pl.multiple_of(slots[b] * ROWS_BACK + f * 8, 8), 8), :]
                blocks.append(jnp.where(land[b] == 0, v, 0.0))
            rows.append(swap_groups(blocks, group))
        for q in range(4):
            at = pl.ds(32 * bx + q, 8, stride=4)
            for f in range(NBACK):
                v = rows[f][q]
                tile[f, at, :] = kept[0, at, :] * v if f == 2 else v
            tile[7, at, :] = kept[1, at, :] * rows[0][q]
        part = pl.ds(32 * bx, 32)
        copies.append(pltpu.make_async_copy(tile.at[:, part, :], out.at[:, part, :], sems.at[bx]))
        copies[-1].start()
    for copy in copies:
        copy.wait()


def unpack(own, land, back, kept):
    return pl.pallas_call(
        unpack_kernel,
        out_shape=jax.ShapeDtypeStruct((8, 128, 128), F32),
        in_specs=[SSPEC, SSPEC, VSPEC, VSPEC],
        out_specs=pl.BlockSpec(memory_space=pl.ANY),
        scratch_shapes=[
            pltpu.VMEM((8, 128, 128), F32),
            pltpu.SMEM((B,), jnp.int32),
            pltpu.SemaphoreType.DMA((4,)),
        ],
        name="unpack",
    )(own, land, *vmem(back, kept))


def prepare_kernel(
    land, vel, stress, drive, weight, pressure, warm, share, floe, drift,
    fields, left, right, up, down, warm0, classes0, sems,
):
    copies = fetches(0, warm, (share, floe, drift), warm0, classes0, sems)
    for copy in copies:
        copy.start()
    group = lax.broadcasted_iota(jnp.int32, (32, 128), 1) // 32
    fields[0:2] = vel[...]
    fields[2:5] = stress[...]
    for bx in range(4):
        at = pl.ds(32 * bx, 32)
        water = jnp.zeros((32, 128), F32)
        for by in range(4):
            water = jnp.where(group == by, (1 - land[4 * bx + by]).astype(F32), water)
        w = weight[at, :]
        scale = water / (w + 0.5)
        beta = 0.5 * scale
        fields[5, at, :] = pressure[at, :] * (1.0 / 3.0)
        fields[6, at, :] = scale * w
        fields[7, at, :] = 0.25 * beta
        fields[8, at, :] = beta * (drive[0, at, :] + drive[2, at, :])
        fields[9, at, :] = beta * (drive[1, at, :] + drive[3, at, :])
    piece = lax.broadcasted_iota(jnp.int32, (8, 128), 1) // 8
    for f in range(NF):
        to_left = jnp.zeros((8, 128), F32)
        to_right = jnp.zeros((8, 128), F32)
        for t in range(16):
            x = fields[f, 8 * t : 8 * t + 8, :]
            to_left = jnp.where(piece == t, turn(x, 8 * t), to_left)
            to_right = jnp.where(piece == t, turn(x, 8 * t + 8), to_right)
        left[f] = to_left
        right[f] = to_right
    up[...] = fields[:, 0:8, :]
    down[...] = fields[:, 120:128, :]
    for copy in copies:
        copy.wait()


def turn(x, shift):
    shift = shift % 128
    return pltpu.roll(x, shift, 1) if shift else x


def prepare(land, vel, stress, drive, weight, pressure, *columns_in):
    edge = pltpu.VMEM((NF, 8, 128), F32)
    return pl.pallas_call(
        prepare_kernel,
        out_shape=(
            jax.ShapeDtypeStruct((NF, 128, 128), F32),
            edge,
            edge,
            edge,
            edge,
            pltpu.VMEM((NCAT, NLAY, 8, CHUNK), F32),
            pltpu.VMEM((3, NCAT, 8, CHUNK), F32),
        ),
        in_specs=[SSPEC] + [VSPEC] * 5 + [HBM] * 4,
        out_specs=(VSPEC,) * 7,
        scratch_shapes=[pltpu.SemaphoreType.DMA((4,))],
        name="prepare",
    )(land, vel, stress, drive, weight, pressure, *columns_in)


def rows_kernel(first_rows, last_rows, left, right, up, down):
    piece = lax.broadcasted_iota(jnp.int32, (8, 128), 1) // 8
    for dst, src, t in ((up, first_rows, 0), (down, last_rows, 15)):
        dst[0:NF] = src[...]
        for i, side in enumerate((left, right)):
            corner = jnp.zeros((8, 128), F32)
            for f in range(NF):
                corner = jnp.where(piece == f, turn(side[f], 8 * (f - t)), corner)
            dst[NF + i] = corner


def edge_rows(first_rows, last_rows, left, right):
    edge = pltpu.VMEM((NF + 2, 8, 128), F32)
    return pl.pallas_call(
        rows_kernel,
        out_shape=(edge, edge),
        in_specs=[VSPEC] * 4,
        out_specs=(VSPEC, VSPEC),
        name="rows",
    )(*vmem(first_rows, last_rows, left, right))


def stage_kernel(fields, _, staged, sem):
    copy = pltpu.make_async_copy(fields, staged, sem)
    copy.start()
    copy.wait()


def stage(fields, after):
    return pl.pallas_call(
        stage_kernel,
        out_shape=pltpu.VMEM((NF, 128, 128), F32),
        in_specs=[HBM, VSPEC],
        out_specs=VSPEC,
        scratch_shapes=[pltpu.SemaphoreType.DMA(())],
        name="stage",
    )(fields, vmem(after))


GUARD = 8


def evp_kernel(fields, left, right, top, bottom, vel_out, stress_out, ext):
    lane = lax.broadcasted_iota(jnp.int32, (8, 128), 1)
    zero = jnp.zeros((8, 128), F32)

    def beside(from_right, from_left):
        return jnp.where(lane < 8, from_right, jnp.where(lane >= 120, from_left, 0.0))

    for f in range(NF):
        for h in range(2):
            ext[f, h, 0:8, :] = zero
            ext[f, h, 152:160, :] = zero
        for edge, r in ((top, 8), (bottom, 144)):
            ext[f, 0, r : r + 8, :] = edge[f]
            ext[f, 1, r : r + 8, :] = beside(
                turn(edge[NF + 1], -8 * f), turn(edge[NF], 120 - 8 * f)
            )
        ext[f, 0, 16:144, :] = fields[f]
        for t in range(16):
            r = 16 + 8 * t
            ext[f, 1, r : r + 8, :] = beside(
                turn(right[f], -8 * t), turn(left[f], 120 - 8 * t)
            )

    def across(x):
        n0, n1 = turn(x[0], 127), turn(x[1], 127)
        p0, p1 = turn(x[0], 1), turn(x[1], 1)
        last = lane == 127
        first = lane == 0
        return (
            jnp.where(last, n1, n0) - jnp.where(first, p1, p0),
            jnp.where(last, n0, n1) - jnp.where(first, p0, p1),
        )

    def subcycle(step, carry):
        for t in range(18):
            r = GUARD + 8 * t
            here, down, up = pl.ds(r, 8), pl.ds(r + 1, 8), pl.ds(r - 1, 8)
            b = across([ext[1, h, here, :] for h in range(2)])
            c = across([ext[0, h, here, :] for h in range(2)])
            for h in range(2):
                a = ext[0, h, down, :] - ext[0, h, up, :]
                d = ext[1, h, down, :] - ext[1, h, up, :]
                plus = a + b[h]
                minus = a - b[h]
                shear = c[h] + d
                square = 0.25 * (plus * plus) + 0.0625 * (minus * minus + shear * shear) + 0.04
                p3 = ext[5, h, here, :]
                k = p3 * lax.rsqrt(square)
                ext[2, h, here, :] = (2.0 / 3.0) * ext[2, h, here, :] + (0.5 * k) * plus - p3
                ext[3, h, here, :] = (2.0 / 3.0) * ext[3, h, here, :] + (0.125 * k) * minus
                ext[4, h, here, :] = (2.0 / 3.0) * ext[4, h, here, :] + (0.0625 * k) * shear
        for t in range(18):
            r = GUARD + 8 * t
            here, down, up = pl.ds(r, 8), pl.ds(r + 1, 8), pl.ds(r - 1, 8)
            shear = across([ext[4, h, here, :] for h in range(2)])
            differ = across([ext[2, h, here, :] - ext[3, h, here, :] for h in range(2)])
            for h in range(2):
                force_x = (ext[2, h, down, :] + ext[3, h, down, :]) - (
                    ext[2, h, up, :] + ext[3, h, up, :]
                )
                force_x = force_x + 2.0 * shear[h]
                force_y = differ[h] + 2.0 * (ext[4, h, down, :] - ext[4, h, up, :])
                alpha = ext[6, h, here, :]
                beta = ext[7, h, here, :]
                east = ext[0, h, here, :]
                north = ext[1, h, here, :]
                ext[0, h, here, :] = (
                    alpha * (east + 0.15 * north) + beta * force_x + ext[8, h, here, :]
                )
                ext[1, h, here, :] = (
                    alpha * (north - 0.15 * east) + beta * force_y + ext[9, h, here, :]
                )
        return carry

    lax.fori_loop(0, SUB, subcycle, 0)
    for f in range(2):
        vel_out[f] = ext[f, 0, 16:144, :]
    for f in range(3):
        stress_out[f] = ext[2 + f, 0, 16:144, :]


def evp(fields, left, right, top, bottom):
    return pl.pallas_call(
        evp_kernel,
        out_shape=(
            jax.ShapeDtypeStruct((2, 128, 128), F32),
            jax.ShapeDtypeStruct((3, 128, 128), F32),
        ),
        in_specs=[VSPEC] * 5,
        out_specs=(VSPEC, VSPEC),
        scratch_shapes=[pltpu.VMEM((NF, 2, 160, 128), F32)],
        name="evp",
    )(*vmem(fields, left, right, top, bottom))


def exchange(axis, to_lower, to_upper):
    peers = lax.axis_size(axis)
    up = [(i, i + 1) for i in range(peers - 1)]
    down = [(i + 1, i) for i in range(peers - 1)]
    from_lower = lax.ppermute(to_upper, axis, up)
    from_upper = lax.ppermute(to_lower, axis, down)
    return from_lower, from_upper


def swap(payload, rows):
    n = lax.axis_size("gy")
    out = lax.all_to_all(
        payload.reshape(n, CAP * rows, 128), "gy", split_axis=0, concat_axis=0, tiled=True
    )
    return out.reshape(n * CAP * rows, 128)


def step(
    conditions,
    warmth,
    share,
    floe,
    drift,
    velocity,
    stress,
    drive,
    weight,
    pressure,
    holder,
    land,
):
    own = holder.reshape(B)
    payload, kept = pack(own, land, conditions)
    recv = swap(payload, ROWS_OUT)

    columns_in = (
        warmth.transpose(1, 2, 0, 3),
        share.transpose(1, 0, 2),
        floe.transpose(1, 0, 2),
        drift.transpose(1, 0, 2),
    )
    fields, to_left, to_right, first, last, warm0, classes0 = prepare(
        land, velocity, stress, drive, weight, pressure, *columns_in
    )
    left, right = exchange("gy", to_left, to_right)

    new_warm, flux = columns(*columns_in, warm0, classes0, recv)
    back = swap(flux, ROWS_BACK)
    first_rows, last_rows = edge_rows(first, last, left, right)
    top, bottom = exchange("gx", first_rows, last_rows)
    fields = stage(fields, first_rows)
    velocity_new, stress_new = evp(fields, left, right, top, bottom)
    exchanges = unpack(own, land, back, kept)
    return (new_warm.transpose(2, 0, 1, 3), exchanges, velocity_new, stress_new)


def solution(mesh):
    return jax.shard_map(
        step,
        mesh=mesh,
        in_specs=(
            P(None, "gx", "gy"),
            P(("gx", "gy"), None, None, None),
            P(("gx", "gy"), None, None),
            P(("gx", "gy"), None, None),
            P(("gx", "gy"), None, None),
            P(None, "gx", "gy"),
            P(None, "gx", "gy"),
            P(None, "gx", "gy"),
            P("gx", "gy"),
            P("gx", "gy"),
            P(("gx", "gy"), None),
            P(("gx", "gy")),
        ),
        out_specs=(
            P(("gx", "gy"), None, None, None),
            P(None, "gx", "gy"),
            P(None, "gx", "gy"),
            P(None, "gx", "gy"),
        ),
        check_vma=False,
    )
```

```python
import jax
import jax.numpy as jnp
from jax import lax
from jax.experimental import pallas as pl
from jax.experimental.pallas import tpu as pltpu
from jax.sharding import PartitionSpec as P


B = 16
CAP = 2
NSEND = 6
NBACK = 7
NF = 10
SUB = 4
NCAT = 5
NLAY = 10
NSNOW = 3
ROWS_OUT = NSEND * 8
ROWS_BACK = NBACK * 8

F32 = jnp.float32
LOG2E = 1.4426950408889634
VSPEC = pl.BlockSpec(memory_space=pltpu.VMEM)
SSPEC = pl.BlockSpec(memory_space=pltpu.SMEM)


def vmem(*arrays):
    out = [pltpu.with_memory_space_constraint(a, pltpu.VMEM) for a in arrays]
    return out if len(out) > 1 else out[0]


def lane_groups():
    return lax.broadcasted_iota(jnp.int32, (8, 128), 1) // 32


def swap_groups(rows, group):
    low = group < 2
    even = (group & 1) == 0
    v0, v1, v2, v3 = rows

    def roll(x, s):
        return pltpu.roll(x, s, 1)

    a0 = jnp.where(low, v0, roll(v2, 64))
    a2 = jnp.where(low, roll(v0, 64), v2)
    a1 = jnp.where(low, v1, roll(v3, 64))
    a3 = jnp.where(low, roll(v1, 64), v3)
    return (
        jnp.where(even, a0, roll(a1, 32)),
        jnp.where(even, roll(a0, 96), a1),
        jnp.where(even, a2, roll(a3, 32)),
        jnp.where(even, roll(a2, 96), a3),
    )


def block_slots(own, land, count, blocks):
    slots = []
    for b in blocks:
        o = own[b]
        r = count[o]
        slots.append(jnp.minimum(o * CAP + r, B * CAP - 1))
        count[o] = r + 1 - land[b]
    return slots


def start_count(count):
    for o in range(B):
        count[o] = 0


def pack_kernel(own, land, x, out, kept, count):
    out[...] = jnp.zeros_like(out)
    kept[0] = 0.7 * x[3]
    kept[1] = -0.05 * x[1]
    start_count(count)
    slots = block_slots(own, land, count, range(B))
    group = lane_groups()
    for bx in range(4):

        def rows(f):
            return [x[f, pl.ds(32 * bx + q, 8, stride=4), :] for q in range(4)]

        visible, near_red, longwave = rows(3), rows(4), rows(5)
        fields = [
            rows(0),
            rows(1),
            rows(2),
            [0.25 * a + 0.45 * b + 0.3 * c for a, b, c in zip(visible, near_red, longwave)],
            rows(6),
            [1.0 / (1.0 + 2.0 * w) for w in rows(7)],
        ]
        blocks = [swap_groups(r, group) for r in fields]
        for by in range(4):
            b = 4 * bx + by

            @pl.when(land[b] == 0)
            def _():
                for f in range(NSEND):
                    out[pl.ds(pl.multiple_of(slots[b] * ROWS_OUT + f * 8, 8), 8), :] = blocks[f][by]


def pack(own, land, conditions):
    return pl.pallas_call(
        pack_kernel,
        out_shape=(pltpu.VMEM((B * CAP * ROWS_OUT, 128), F32), pltpu.VMEM((2, 128, 128), F32)),
        in_specs=[SSPEC, SSPEC, VSPEC],
        out_specs=(VSPEC, VSPEC),
        scratch_shapes=[pltpu.SMEM((B,), jnp.int32)],
        name="pack",
    )(own, land, conditions)


def one_column(temps, share, floe, snow_depth, forcing, sig):
    ocean, air, source_top, top_resist = forcing
    h14 = floe * (1.0 / 14.0)
    h27 = floe * (2.0 / 7.0)
    h47 = floe * (4.0 / 7.0)
    m_snow = snow_depth * (2.0 / 3.0)
    half_snow = snow_depth * (0.5 / 0.9)
    g_snow = 0.9 / snow_depth
    g_top = 1.0 / (half_snow + top_resist)
    inv_cond = []
    mass = [m_snow] * NSNOW
    for j in range(NLAY - NSNOW):
        t = temps[NSNOW + j]
        inv_cond.append(1.0 / (2.0 + sig[j] / (t - 0.5)))
        mass.append(h27 + h47 * (sig[j] / (t * t + 0.1)))
    cond = [g_snow, g_snow, 1.0 / (half_snow + h14 * inv_cond[0])]
    for j in range(NLAY - NSNOW - 1):
        cond.append(1.0 / (h14 * (inv_cond[j] + inv_cond[j + 1])))
    g_bot = 1.0 / (h14 * inv_cond[-1])
    ratios = []
    values = []
    u = mass[0] + g_top
    held = mass[0] * temps[0]
    y = held + g_top * air + source_top
    for l in range(NLAY):
        below = cond[l] if l < NLAY - 1 else g_bot
        pivot = 1.0 / (u + below)
        ratio = below * pivot
        if l < NLAY - 1:
            ratios.append(ratio)
            values.append(y * pivot)
            u = mass[l + 1] + ratio * u
            mt = mass[l + 1] * temps[l + 1]
            held = held + mt
            y = mt + ratio * y
        else:
            last = y * pivot + ratio * ocean
    solved = [last]
    for l in range(NLAY - 2, -1, -1):
        solved.insert(0, values[l] + ratios[l] * solved[0])
    bottom = share * (g_bot * (last - ocean))
    top = share * (g_top * (air - solved[0]))
    light = share * jnp.exp2((-5.0 * LOG2E) * snow_depth - (1.5 * LOG2E) * floe)
    return solved, (
        bottom,
        top,
        light,
        share * solved[0],
        share * snow_depth,
        share * floe,
        share * held,
        share,
    )


HBM = pl.BlockSpec(memory_space=pltpu.HBM)
CHUNKS = 8
CHUNK = 512


def chunk_at(s):
    rows = pl.ds(pl.multiple_of(s // 2 * 8, 8), 8)
    lanes = pl.ds(pl.multiple_of(s % 2 * CHUNK, CHUNK), CHUNK)
    return rows, lanes


def fetches(s, warm, classes, warm_to, classes_to, sems):
    rows, lanes = chunk_at(s)
    return [pltpu.make_async_copy(warm.at[:, :, rows, lanes], warm_to, sems.at[3])] + [
        pltpu.make_async_copy(src.at[:, rows, lanes], classes_to.at[i], sems.at[i])
        for i, src in enumerate(classes)
    ]


def column_kernel(
    warm, share, floe, drift, warm0, classes0, recv, new_warm, flux, wbuf, cbuf, obuf, fbuf, insem, outsem, fsem
):
    classes = (share, floe, drift)

    def fetch(s, slot):
        return fetches(s, warm, classes, wbuf.at[slot], cbuf.at[slot], insem.at[slot])

    def put(s, slot):
        rows, lanes = chunk_at(s)
        return pltpu.make_async_copy(obuf.at[slot], new_warm.at[:, :, rows, lanes], outsem.at[slot])

    def put_flux(g):
        part = pl.ds(pl.multiple_of(g * 8 * ROWS_BACK, 8), 8 * ROWS_BACK)
        return pltpu.make_async_copy(fbuf.at[part, :], flux.at[part, :], fsem.at[g])

    def compute(s, warm_in, classes_in, out):
        first = s // 2 * 8

        def tile(k, carry):
            kk = s % 2 * 4 + k
            lanes = pl.ds(pl.multiple_of(k * 128, 128), 128)

            def field(f):
                return recv[pl.ds(first * ROWS_OUT + f * 8 + kk, 8, stride=ROWS_OUT), :]

            ocean, salinity, air, source_top, snowfall, top_resist = [
                field(f) for f in range(NSEND)
            ]
            filled = salinity > 0.25
            sig = [salinity * (0.02 + 0.01 * j) for j in range(NLAY - NSNOW)]
            snow_add = 0.3 * snowfall
            sums = None
            for c in range(NCAT):
                temps = [warm_in[c, l, :, lanes] for l in range(NLAY)]
                solved, terms = one_column(
                    temps,
                    classes_in[0, c, :, lanes],
                    classes_in[1, c, :, lanes],
                    classes_in[2, c, :, lanes] + snow_add,
                    (ocean, air, source_top, top_resist),
                    sig,
                )
                for l in range(NLAY):
                    out[c, l, :, lanes] = jnp.where(filled, solved[l], temps[l])
                sums = terms if sums is None else tuple(a + b for a, b in zip(sums, terms))
            bottom, top, light, surface, snow, thick, held, total = sums
            back = (
                bottom,
                top,
                light,
                surface,
                snow,
                thick - 0.05 * bottom,
                0.05 * (held + top - bottom + source_top * total),
            )
            for f in range(NBACK):
                fbuf[pl.ds(first * ROWS_BACK + f * 8 + kk, 8, stride=ROWS_BACK), :] = back[f]
            return carry

        lax.fori_loop(0, 4, tile, 0, unroll=True)

    def start(copies):
        for copy in copies:
            copy.start()

    def wait(copies):
        for copy in copies:
            copy.wait()

    start(fetch(1, 1))
    start(fetch(2, 0))
    compute(0, warm0, classes0, obuf.at[0])
    put(0, 0).start()

    for s in range(1, CHUNKS):
        slot = s % 2
        wait(fetch(s, slot))
        if s >= 2:
            put(s - 2, slot).wait()
        compute(s, wbuf.at[slot], cbuf.at[slot], obuf.at[slot])
        put(s, slot).start()
        if slot == 1:
            put_flux(s // 2).start()
        if s + 2 < CHUNKS:
            start(fetch(s + 2, slot))
    put(CHUNKS - 2, 0).wait()
    put(CHUNKS - 1, 1).wait()
    for g in range(CHUNKS // 2):
        put_flux(g).wait()


def columns(warm, share, floe, drift, warm0, classes0, recv):
    return pl.pallas_call(
        column_kernel,
        out_shape=(
            jax.ShapeDtypeStruct((NCAT, NLAY, 32, 1024), F32),
            jax.ShapeDtypeStruct((B * CAP * ROWS_BACK, 128), F32),
        ),
        in_specs=[HBM] * 4 + [VSPEC] * 3,
        out_specs=(HBM, HBM),
        scratch_shapes=[
            pltpu.VMEM((2, NCAT, NLAY, 8, CHUNK), F32),
            pltpu.VMEM((2, 3, NCAT, 8, CHUNK), F32),
            pltpu.VMEM((2, NCAT, NLAY, 8, CHUNK), F32),
            pltpu.VMEM((B * CAP * ROWS_BACK, 128), F32),
            pltpu.SemaphoreType.DMA((2, 4)),
            pltpu.SemaphoreType.DMA((2,)),
            pltpu.SemaphoreType.DMA((4,)),
        ],
        name="columns",
    )(warm, share, floe, drift, *vmem(warm0, classes0, recv))


def unpack_kernel(own, land, back, kept, out, tile, count, sems):
    start_count(count)
    slots = block_slots(own, land, count, range(B))
    group = lane_groups()
    copies = []
    for bx in range(4):
        rows = []
        for f in range(NBACK):
            blocks = []
            for b in range(4 * bx, 4 * bx + 4):
                v = back[pl.ds(pl.multiple_of(slots[b] * ROWS_BACK + f * 8, 8), 8), :]
                blocks.append(jnp.where(land[b] == 0, v, 0.0))
            rows.append(swap_groups(blocks, group))
        for q in range(4):
            at = pl.ds(32 * bx + q, 8, stride=4)
            for f in range(NBACK):
                v = rows[f][q]
                tile[f, at, :] = kept[0, at, :] * v if f == 2 else v
            tile[7, at, :] = kept[1, at, :] * rows[0][q]
        part = pl.ds(32 * bx, 32)
        copies.append(pltpu.make_async_copy(tile.at[:, part, :], out.at[:, part, :], sems.at[bx]))
        copies[-1].start()
    for copy in copies:
        copy.wait()


def unpack(own, land, back, kept):
    return pl.pallas_call(
        unpack_kernel,
        out_shape=jax.ShapeDtypeStruct((8, 128, 128), F32),
        in_specs=[SSPEC, SSPEC, VSPEC, VSPEC],
        out_specs=pl.BlockSpec(memory_space=pl.ANY),
        scratch_shapes=[
            pltpu.VMEM((8, 128, 128), F32),
            pltpu.SMEM((B,), jnp.int32),
            pltpu.SemaphoreType.DMA((4,)),
        ],
        name="unpack",
    )(own, land, *vmem(back, kept))


def prepare_kernel(
    land, vel, stress, drive, weight, pressure, warm, share, floe, drift,
    fields, left, right, up, down, warm0, classes0, sems,
):
    copies = fetches(0, warm, (share, floe, drift), warm0, classes0, sems)
    for copy in copies:
        copy.start()
    group = lax.broadcasted_iota(jnp.int32, (32, 128), 1) // 32
    fields[0:2] = vel[...]
    fields[2:5] = stress[...]
    for bx in range(4):
        at = pl.ds(32 * bx, 32)
        water = jnp.zeros((32, 128), F32)
        for by in range(4):
            water = jnp.where(group == by, (1 - land[4 * bx + by]).astype(F32), water)
        w = weight[at, :]
        scale = water / (w + 0.5)
        beta = 0.5 * scale
        fields[5, at, :] = pressure[at, :] * (1.0 / 3.0)
        fields[6, at, :] = scale * w
        fields[7, at, :] = 0.25 * beta
        fields[8, at, :] = beta * (drive[0, at, :] + drive[2, at, :])
        fields[9, at, :] = beta * (drive[1, at, :] + drive[3, at, :])
    piece = lax.broadcasted_iota(jnp.int32, (8, 128), 1) // 8
    for f in range(NF):
        to_left = jnp.zeros((8, 128), F32)
        to_right = jnp.zeros((8, 128), F32)
        for t in range(16):
            x = fields[f, 8 * t : 8 * t + 8, :]
            to_left = jnp.where(piece == t, turn(x, 8 * t), to_left)
            to_right = jnp.where(piece == t, turn(x, 8 * t + 8), to_right)
        left[f] = to_left
        right[f] = to_right
    up[...] = fields[:, 0:8, :]
    down[...] = fields[:, 120:128, :]
    for copy in copies:
        copy.wait()


def turn(x, shift):
    shift = shift % 128
    return pltpu.roll(x, shift, 1) if shift else x


def prepare(land, vel, stress, drive, weight, pressure, *columns_in):
    edge = pltpu.VMEM((NF, 8, 128), F32)
    return pl.pallas_call(
        prepare_kernel,
        out_shape=(
            jax.ShapeDtypeStruct((NF, 128, 128), F32),
            edge,
            edge,
            edge,
            edge,
            pltpu.VMEM((NCAT, NLAY, 8, CHUNK), F32),
            pltpu.VMEM((3, NCAT, 8, CHUNK), F32),
        ),
        in_specs=[SSPEC] + [VSPEC] * 5 + [HBM] * 4,
        out_specs=(VSPEC,) * 7,
        scratch_shapes=[pltpu.SemaphoreType.DMA((4,))],
        name="prepare",
    )(land, vel, stress, drive, weight, pressure, *columns_in)


def rows_kernel(first_rows, last_rows, left, right, up, down):
    piece = lax.broadcasted_iota(jnp.int32, (8, 128), 1) // 8
    for dst, src, t in ((up, first_rows, 0), (down, last_rows, 15)):
        dst[0:NF] = src[...]
        for i, side in enumerate((left, right)):
            corner = jnp.zeros((8, 128), F32)
            for f in range(NF):
                corner = jnp.where(piece == f, turn(side[f], 8 * (f - t)), corner)
            dst[NF + i] = corner


def edge_rows(first_rows, last_rows, left, right):
    edge = pltpu.VMEM((NF + 2, 8, 128), F32)
    return pl.pallas_call(
        rows_kernel,
        out_shape=(edge, edge),
        in_specs=[VSPEC] * 4,
        out_specs=(VSPEC, VSPEC),
        name="rows",
    )(*vmem(first_rows, last_rows, left, right))


def stage_kernel(fields, _, staged, sem):
    copy = pltpu.make_async_copy(fields, staged, sem)
    copy.start()
    copy.wait()


def stage(fields, after):
    return pl.pallas_call(
        stage_kernel,
        out_shape=pltpu.VMEM((NF, 128, 128), F32),
        in_specs=[HBM, VSPEC],
        out_specs=VSPEC,
        scratch_shapes=[pltpu.SemaphoreType.DMA(())],
        name="stage",
    )(fields, vmem(after))


GUARD = 8


def evp_kernel(fields, left, right, top, bottom, vel_out, stress_out, ext):
    lane = lax.broadcasted_iota(jnp.int32, (8, 128), 1)
    zero = jnp.zeros((8, 128), F32)

    def beside(from_right, from_left):
        return jnp.where(lane < 8, from_right, jnp.where(lane >= 120, from_left, 0.0))

    for f in range(NF):
        for h in range(2):
            ext[f, h, 0:8, :] = zero
            ext[f, h, 152:160, :] = zero
        for edge, r in ((top, 8), (bottom, 144)):
            ext[f, 0, r : r + 8, :] = edge[f]
            ext[f, 1, r : r + 8, :] = beside(
                turn(edge[NF + 1], -8 * f), turn(edge[NF], 120 - 8 * f)
            )
        ext[f, 0, 16:144, :] = fields[f]
        for t in range(16):
            r = 16 + 8 * t
            ext[f, 1, r : r + 8, :] = beside(
                turn(right[f], -8 * t), turn(left[f], 120 - 8 * t)
            )

    def across(x):
        n0, n1 = turn(x[0], 127), turn(x[1], 127)
        p0, p1 = turn(x[0], 1), turn(x[1], 1)
        last = lane == 127
        first = lane == 0
        return (
            jnp.where(last, n1, n0) - jnp.where(first, p1, p0),
            jnp.where(last, n0, n1) - jnp.where(first, p0, p1),
        )

    def subcycle(step, carry):
        for t in range(18):
            r = GUARD + 8 * t
            here, down, up = pl.ds(r, 8), pl.ds(r + 1, 8), pl.ds(r - 1, 8)
            b = across([ext[1, h, here, :] for h in range(2)])
            c = across([ext[0, h, here, :] for h in range(2)])
            for h in range(2):
                a = ext[0, h, down, :] - ext[0, h, up, :]
                d = ext[1, h, down, :] - ext[1, h, up, :]
                plus = a + b[h]
                minus = a - b[h]
                shear = c[h] + d
                square = 0.25 * (plus * plus) + 0.0625 * (minus * minus + shear * shear) + 0.04
                p3 = ext[5, h, here, :]
                k = p3 * lax.rsqrt(square)
                ext[2, h, here, :] = (2.0 / 3.0) * ext[2, h, here, :] + (0.5 * k) * plus - p3
                ext[3, h, here, :] = (2.0 / 3.0) * ext[3, h, here, :] + (0.125 * k) * minus
                ext[4, h, here, :] = (2.0 / 3.0) * ext[4, h, here, :] + (0.0625 * k) * shear
        for t in range(18):
            r = GUARD + 8 * t
            here, down, up = pl.ds(r, 8), pl.ds(r + 1, 8), pl.ds(r - 1, 8)
            shear = across([ext[4, h, here, :] for h in range(2)])
            differ = across([ext[2, h, here, :] - ext[3, h, here, :] for h in range(2)])
            for h in range(2):
                force_x = (ext[2, h, down, :] + ext[3, h, down, :]) - (
                    ext[2, h, up, :] + ext[3, h, up, :]
                )
                force_x = force_x + 2.0 * shear[h]
                force_y = differ[h] + 2.0 * (ext[4, h, down, :] - ext[4, h, up, :])
                alpha = ext[6, h, here, :]
                beta = ext[7, h, here, :]
                east = ext[0, h, here, :]
                north = ext[1, h, here, :]
                ext[0, h, here, :] = (
                    alpha * (east + 0.15 * north) + beta * force_x + ext[8, h, here, :]
                )
                ext[1, h, here, :] = (
                    alpha * (north - 0.15 * east) + beta * force_y + ext[9, h, here, :]
                )
        return carry

    lax.fori_loop(0, SUB, subcycle, 0)
    for f in range(2):
        vel_out[f] = ext[f, 0, 16:144, :]
    for f in range(3):
        stress_out[f] = ext[2 + f, 0, 16:144, :]


def evp(fields, left, right, top, bottom):
    return pl.pallas_call(
        evp_kernel,
        out_shape=(
            jax.ShapeDtypeStruct((2, 128, 128), F32),
            jax.ShapeDtypeStruct((3, 128, 128), F32),
        ),
        in_specs=[VSPEC] * 5,
        out_specs=(VSPEC, VSPEC),
        scratch_shapes=[pltpu.VMEM((NF, 2, 160, 128), F32)],
        name="evp",
    )(*vmem(fields, left, right, top, bottom))


def exchange(axis, to_lower, to_upper):
    peers = lax.axis_size(axis)
    up = [(i, i + 1) for i in range(peers - 1)]
    down = [(i + 1, i) for i in range(peers - 1)]
    from_lower = lax.ppermute(to_upper, axis, up)
    from_upper = lax.ppermute(to_lower, axis, down)
    return from_lower, from_upper


def swap(payload, rows):
    n = lax.axis_size("gy")
    out = lax.all_to_all(
        payload.reshape(n, CAP * rows, 128), "gy", split_axis=0, concat_axis=0, tiled=True
    )
    return out.reshape(n * CAP * rows, 128)


def step(
    conditions,
    warmth,
    share,
    floe,
    drift,
    velocity,
    stress,
    drive,
    weight,
    pressure,
    holder,
    land,
):
    own = holder.reshape(B)
    payload, kept = pack(own, land, conditions)
    recv = swap(payload, ROWS_OUT)

    columns_in = (
        warmth.transpose(1, 2, 0, 3),
        share.transpose(1, 0, 2),
        floe.transpose(1, 0, 2),
        drift.transpose(1, 0, 2),
    )
    fields, to_left, to_right, first, last, warm0, classes0 = prepare(
        land, velocity, stress, drive, weight, pressure, *columns_in
    )
    left, right = exchange("gy", to_left, to_right)

    new_warm, flux = columns(*columns_in, warm0, classes0, recv)
    back = swap(flux, ROWS_BACK)
    first_rows, last_rows = edge_rows(first, last, left, right)
    top, bottom = exchange("gx", first_rows, last_rows)
    fields = stage(fields, first_rows)
    velocity_new, stress_new = evp(fields, left, right, top, bottom)
    exchanges = unpack(own, land, back, kept)
    return (new_warm.transpose(2, 0, 1, 3), exchanges, velocity_new, stress_new)


def solution(mesh):
    return jax.shard_map(
        step,
        mesh=mesh,
        in_specs=(
            P(None, "gx", "gy"),
            P(("gx", "gy"), None, None, None),
            P(("gx", "gy"), None, None),
            P(("gx", "gy"), None, None),
            P(("gx", "gy"), None, None),
            P(None, "gx", "gy"),
            P(None, "gx", "gy"),
            P(None, "gx", "gy"),
            P("gx", "gy"),
            P("gx", "gy"),
            P(("gx", "gy"), None),
            P(("gx", "gy")),
        ),
        out_specs=(
            P(("gx", "gy"), None, None, None),
            P(None, "gx", "gy"),
            P(None, "gx", "gy"),
            P(None, "gx", "gy"),
        ),
        check_vma=False,
    )
```
